512 devices in a mesh: sec: 32 (over y, z_hi, core), sub: 16 (over z_lo, x).
Axes of the slice: x: 4, y: 8, z: 8 (z_hi: 2, z_lo: 4; z = z_hi * 4 + z_lo), core: 2. Of those that a mesh axis runs over, the one named last changes fastest.
Arguments:
- forcing: float32 [32, 192, 64, 128], P('sec', 'sub'), may hold values from -60 to 60
- coupling: float32 [32, 192, 64, 128], P('sec', 'sub'), may hold values from -0.6 to 0.6
- diag_pair: float32 [32, 192, 64, 128], P('sec', 'sub'), may hold values from -1 to 9
- side: float32 [32, 192, 32], P('sec', 'sub'), may hold values from -1 to -0.3
- basis: float32 [32, 1024, 768], P('sec', 'sub'), may hold values from -0.21875 to 0.21875
- coarse_inverse: float32 [32, 1024, 1024], P('sec', 'sub'), may hold values from -0.05 to 0.3
Outputs:
- solution: float32 [32, 192, 64, 128], P('sec', 'sub')
The draws below stay inside these ranges and needn't reach their ends.
All inputs are finite; a program needn't handle non-finite values.
Results may differ from the reference program's by a relative error of at most 0.0001.
Values sent between devices are 32-bit elements; how exact they have to be, the bound alone decides.
No kernel may reach another device: no remote copies, remote signals or barrier semaphores. Data moves between devices by JAX's collectives and lax.ppermute only.
A program may use at most 64 MiB of HBM per device.

```python
import math
import jax
import jax.numpy as jnp
import numpy as np
from jax import lax

NODES = 64
FACE = 16
COLS = 128
COARSE = 1024
NB = 12
SWEEPS = 4
ITERS = 2
SECTIONS = 32
BLOCKS = 192
N_SUB = 16


def draw_forcing(key, part):
    full_shape = (SECTIONS, BLOCKS, NODES, COLS)
    section_pos = jnp.arange(SECTIONS, dtype=jnp.float32).reshape(SECTIONS, 1, 1, 1) / max(SECTIONS - 1, 1)
    block_pos = jnp.arange(BLOCKS, dtype=jnp.float32).reshape(1, BLOCKS, 1, 1) / max(BLOCKS - 1, 1)
    weight_field = jnp.exp(section_pos * math.log(3.0) + block_pos * math.log(4.0))
    values = jnp.clip(jax.random.normal(key, full_shape, jnp.float32), -5.0, 5.0)
    return values * weight_field


def draw_diag_pair(key, part):
    key_main, key_extra = jax.random.split(key)
    full_shape = (SECTIONS, BLOCKS, NODES, NODES)
    identity = jnp.eye(NODES, dtype=jnp.float32)
    direct_part = 8.0 * identity + 0.125 * jnp.clip(jax.random.normal(key_main, full_shape, jnp.float32), -6.0, 6.0)
    inverse_part = 0.125 * identity + 0.006 * jnp.clip(jax.random.normal(key_extra, full_shape, jnp.float32), -6.0, 6.0)
    return jnp.concatenate([direct_part, inverse_part], axis=-1)


def draw_coarse_inverse(key, part):
    full_shape = (SECTIONS, COARSE, COARSE)
    identity = jnp.eye(COARSE, dtype=jnp.float32)
    return 0.25 * identity + 0.008 * jnp.clip(jax.random.normal(key, full_shape, jnp.float32), -6.0, 6.0)


def level_of(rng, dims, cuts, smallest, high):
    level, own = 1.0, jax.random.fold_in(rng, 6)
    for axis_at, parts in cuts:
        heights = jnp.exp(jax.random.uniform(jax.random.fold_in(own, axis_at), (parts,), jnp.float32, smallest / len(cuts), high / len(cuts)))
        level = level * jnp.repeat(heights, dims[axis_at] // parts).reshape([-1 if axis == axis_at else 1 for axis in range(len(dims))])
    return level


def centred(rng, shape, spread, most, shards=(), kind=jnp.bfloat16):
    loudness = level_of(rng, shape, shards, -0.22, 0.18) if shards else 1.0
    drawn = jax.random.normal(rng, shape, jnp.float32) * spread * loudness
    return jnp.minimum(jnp.maximum(drawn, -most), most).astype(kind)


def setup_inputs(seed: int = 0) -> dict:
    key_of = jax.random.split(jax.random.key(seed), 7)
    forcing = draw_forcing(jax.random.fold_in(key_of[6], 71), 0)
    coupling = centred(key_of[1], (SECTIONS, BLOCKS, NODES, 2 * NODES), 0.1, 0.6, ((0, 32), (1, 16)), jnp.float32)
    diag_pair = draw_diag_pair(jax.random.fold_in(key_of[6], 71), 0)
    side = jnp.clip(-1.0 + 0.7 * jax.random.uniform(key_of[3], (SECTIONS, BLOCKS, 2 * FACE), jnp.float32) ** level_of(key_of[3], (SECTIONS, BLOCKS, 2 * FACE), ((0, 32), (1, 16)), -0.2, 0.2), -1.0, -0.3)
    basis = centred(key_of[4], (SECTIONS, COARSE, NB * NODES), (NB * NODES) ** -0.5, 0.21875, ((0, 32), (1, 16)), jnp.float32)
    coarse_inverse = draw_coarse_inverse(jax.random.fold_in(key_of[6], 71), 0)
    return dict(forcing=forcing, coupling=coupling, diag_pair=diag_pair, side=side, basis=basis, coarse_inverse=coarse_inverse)


PRECISE = lax.Precision.HIGHEST


def tile_apply(tile_set, vector):
    return jnp.einsum("bij,bjc->bic", tile_set, vector, precision=PRECISE)


def couple(coupling, diagonal, centre, before, after):
    return tile_apply(diagonal, centre) + tile_apply(coupling, jnp.concatenate([before, after], axis=1))


def chain_apply(coupling, diagonal, vector):
    zero_block = jnp.zeros_like(vector[:1])
    before = jnp.concatenate([zero_block, vector[:-1]], axis=0)
    after = jnp.concatenate([vector[1:], zero_block], axis=0)
    return couple(coupling, diagonal, vector, before, after)


def add_faces(linear, sides, below, above):
    face_rows = sides.shape[-1] // 2
    node_count = linear.shape[1]
    lower_term = sides[:, :face_rows, None] * below
    upper_term = sides[:, face_rows:, None] * above
    return jnp.concatenate([linear[:, :face_rows] + lower_term, linear[:, face_rows:node_count - face_rows], linear[:, node_count - face_rows:] + upper_term], axis=1)


def local_sweeps(residual_ext, coupling_ext, diagonal_ext, inverse_ext):
    update = tile_apply(inverse_ext, residual_ext)
    for sweep_index in range(SWEEPS - 1):
        update = update + tile_apply(inverse_ext, residual_ext - chain_apply(coupling_ext, diagonal_ext, update))
    return update[1:-1]


def precondition_section(operands):
    residual_sec, coupling_sec, pair_sec, basis_sec, inverse_sec = operands
    node_count = residual_sec.shape[1]
    column_count = residual_sec.shape[2]
    window_index = np.arange(N_SUB)[:, None] * NB + np.arange(NB + 2)[None, :]

    def windows(field):
        padded = jnp.concatenate([jnp.zeros_like(field[:1]), field, jnp.zeros_like(field[:1])], axis=0)
        return padded[window_index]

    residual_win = windows(residual_sec)
    tiles_win = windows(jnp.concatenate([coupling_sec, pair_sec], axis=2))
    local_part = jax.vmap(local_sweeps)(residual_win, tiles_win[..., :2 * node_count], tiles_win[..., 2 * node_count:3 * node_count], tiles_win[..., 3 * node_count:])
    local_part = local_part.reshape(residual_sec.shape)
    per_sub = COARSE // N_SUB
    basis_split = basis_sec.reshape(N_SUB, per_sub, NB * node_count)
    field_split = residual_sec.reshape(N_SUB, NB * node_count, column_count)
    projected = jnp.einsum("jkm,jmc->jkc", basis_split, field_split, precision=PRECISE).reshape(COARSE, column_count)
    correction = jnp.dot(inverse_sec, projected, precision=PRECISE).reshape(N_SUB, per_sub, column_count)
    expanded = jnp.einsum("jkm,jkc->jmc", basis_split, correction, precision=PRECISE).reshape(residual_sec.shape)
    return local_part + expanded


def operate_all(field, coupling, diag_pair, side):
    face_rows = side.shape[-1] // 2
    node_count = field.shape[2]
    north_face = field[:, :, node_count - face_rows:]
    south_face = field[:, :, :face_rows]
    below = jnp.concatenate([jnp.zeros_like(north_face[:1]), north_face[:-1]], axis=0)
    above = jnp.concatenate([south_face[1:], jnp.zeros_like(south_face[:1])], axis=0)

    def one_section(operands):
        vector, coupling_sec, pair_sec, sides, lower_in, upper_in = operands
        return add_faces(chain_apply(coupling_sec, pair_sec[:, :, :node_count], vector), sides, lower_in, upper_in)

    return lax.map(one_section, (field, coupling, diag_pair, side, below, above))


def reference(forcing, coupling, diag_pair, side, basis, coarse_inverse):
    residual = forcing
    solution = jnp.zeros_like(forcing)
    for iteration in range(ITERS):
        update = lax.map(precondition_section, (residual, coupling, diag_pair, basis, coarse_inverse))
        image = operate_all(update, coupling, diag_pair, side)
        numerator = jnp.einsum("sbnc,sbnc->c", image, residual, precision=PRECISE)
        denominator = jnp.einsum("sbnc,sbnc->c", image, image, precision=PRECISE)
        step_size = numerator / denominator
        solution = solution + step_size * update
        residual = residual - step_size * image
    return solution
```

```python
import jax
import jax.numpy as jnp
from jax import lax
from jax.sharding import PartitionSpec as P

SWEEPS = 4
SCALE = 2.0**-16

PRECISE = lax.Precision.HIGHEST


def tile_apply(tile_set, vector, precision=PRECISE):
    return jnp.einsum("bij,bjc->bic", tile_set, vector, precision=precision)


def from_neighbours(to_next, to_previous, axis):
    count = lax.axis_size(axis)
    forward = [(i, i + 1) for i in range(count - 1)]
    backward = [(i + 1, i) for i in range(count - 1)]
    return lax.ppermute(to_next, axis, forward), lax.ppermute(to_previous, axis, backward)


def swapped_sections(to_next, to_previous):
    count = lax.axis_size("sec")
    near = [(i, i ^ 1) for i in range(count)]
    low = [(i, i + 1) for i in range(1, count - 1, 2)]
    far = low + [(target, source) for source, target in low]
    even = lax.axis_index("sec") % 2 == 0
    from_far = lax.ppermute(jnp.where(even, to_previous, to_next), "sec", far)
    from_near = lax.ppermute(jnp.where(even, to_next, to_previous), "sec", near)
    return jnp.where(even, from_far, from_near), jnp.where(even, from_near, from_far)


def gather_sub(value):
    count = lax.axis_size("sub")
    spread = jnp.broadcast_to(value[None], (count, *value.shape))
    got = lax.all_to_all(spread, "sub", 0, 0, tiled=True)
    return got.reshape(count * value.shape[0], *value.shape[1:])


def total(sums):
    shape = sums.shape
    flat = sums.reshape(1, -1)
    sections, subs = lax.axis_size("sec"), lax.axis_size("sub")
    pairs = [[2 * g, 2 * g + 1] for g in range(sections // 2)]
    alike = [[2 * g + p for g in range(sections // 2)] for p in range(2)]
    flat = jnp.sum(lax.all_gather(flat, "sec", axis_index_groups=pairs), axis=0)
    spread = jnp.broadcast_to(flat[None], (sections // 2, *flat.shape))
    flat = jnp.sum(lax.all_to_all(spread, "sec", 0, 0, axis_index_groups=alike, tiled=True), axis=0)
    spread = jnp.broadcast_to(flat[None], (subs, *flat.shape))
    flat = jnp.sum(lax.all_to_all(spread, "sub", 0, 0, tiled=True), axis=0)
    return flat.reshape(shape)


def triple(before, vector, after):
    previous = jnp.concatenate([before, vector[:-1]], axis=0)
    following = jnp.concatenate([vector[1:], after], axis=0)
    return jnp.concatenate([previous, following, vector], axis=1)


def shards(forcing, coupling, diag_pair, side, basis, coarse_inverse):
    residual = forcing[0]
    sides = side[0]
    basis_rows = basis[0]
    inverse_rows = coarse_inverse[0]
    nodes, columns = residual.shape[1:]
    faces = sides.shape[1] // 2
    inverses = diag_pair[0, :, :, nodes:]
    tiles = jnp.concatenate([coupling[0], diag_pair[0, :, :, :nodes]], axis=2)
    identity = jnp.concatenate(
        [jnp.zeros((nodes, 2 * nodes), jnp.float32), jnp.eye(nodes, dtype=jnp.float32)], axis=1
    )
    sweep = identity[None] - tile_apply(inverses, tiles)
    zero = jnp.zeros_like(residual[:1])
    low_sweep, high_sweep = from_neighbours(sweep[-1:, :, nodes:], jnp.concatenate([sweep[:1, :, :nodes], sweep[:1, :, 2 * nodes :]], axis=2), "sub")
    gap = jnp.zeros((1, nodes, nodes), jnp.float32)
    low_sweep = jnp.concatenate([gap, low_sweep], axis=2)
    high_sweep = jnp.concatenate([high_sweep[:, :, :nodes], gap, high_sweep[:, :, nodes:]], axis=2)
    sweep_ext = jnp.concatenate([low_sweep, sweep, high_sweep], axis=0)

    def precondition(field):
        start = tile_apply(inverses, field)
        low, high = from_neighbours(start[-1:], start[:1], "sub")
        projected = jnp.dot(basis_rows, field.reshape(-1, columns), precision=PRECISE)
        gathered = gather_sub(projected)
        start = jnp.concatenate([low, start, high], axis=0)
        update = start
        for _ in range(SWEEPS - 1):
            update = start + tile_apply(sweep_ext, triple(zero, update, zero))
        correction = jnp.dot(inverse_rows, gathered, precision=PRECISE)
        expanded = lax.dot_general(basis_rows, correction, (((0,), (0,)), ((), ())), precision=PRECISE)
        return update[1:-1] + expanded.reshape(field.shape)

    def operate(update):
        below, above = swapped_sections(update[:, nodes - faces :], update[:, :faces])
        before, after = from_neighbours(update[-1:], update[:1], "sub")
        linear = tile_apply(tiles, triple(before, update, after))
        lower = sides[:, :faces, None] * below
        upper = sides[:, faces:, None] * above
        return jnp.concatenate(
            [linear[:, :faces] + lower, linear[:, faces : nodes - faces], linear[:, nodes - faces :] + upper],
            axis=1,
        )

    first = precondition(residual)
    image = operate(first)
    rest = residual - image
    second = precondition(rest)
    change = operate(second) * SCALE

    def inner(left, right):
        return jnp.sum(left * right, axis=(0, 1))

    sums = total(
        jnp.stack(
            [inner(image, rest), inner(image, image), inner(change, rest), inner(change, image), inner(change, change)]
        )
    )
    short = -sums[0] / sums[1]
    step = 1.0 - short
    upper = step * (sums[2] + short * sums[3])
    scaled = step / SCALE
    lower = short * short * sums[1] + 2.0 * short * scaled * sums[3] + scaled * scaled * sums[4]
    step_next = upper / SCALE / lower
    result = (step + step_next * short) * first + (step_next * step) * second
    return result[None]


def solution(mesh):
    placed = (
        P("sec", "sub", None, None),
        P("sec", "sub", None, None),
        P("sec", "sub", None, None),
        P("sec", "sub", None),
        P("sec", "sub", None),
        P("sec", "sub", None),
    )
    return jax.shard_map(
        shards, mesh=mesh, in_specs=placed, out_specs=P("sec", "sub", None, None), check_vma=False
    )
```

```python
import jax
import jax.numpy as jnp
from jax import lax
from jax.experimental import pallas as pl
from jax.experimental.pallas import tpu as pltpu
from jax.sharding import PartitionSpec as P

SWEEPS = 4
SCALE = 2.0**-16

PRECISE = lax.Precision.HIGHEST


def dot(left, right):
    return jnp.dot(left, right, precision=PRECISE, preferred_element_type=jnp.float32)


def pairings(axis):
    count = lax.axis_size(axis)
    near = [(i, i ^ 1) for i in range(count)]
    low = [(i, i + 1) for i in range(1, count - 1, 2)]
    return near, low + [(target, source) for source, target in low]


def swap(to_near, to_far, axis):
    near, far = pairings(axis)
    from_far = lax.ppermute(to_far, axis, far)
    return lax.ppermute(to_near, axis, near), from_far


def gather_sub(spread):
    return lax.all_to_all(spread, "sub", 0, 0, tiled=True).reshape(-1, *spread.shape[2:])


def total(sums):
    shape = sums.shape
    flat = sums.reshape(1, -1)
    sections, subs = lax.axis_size("sec"), lax.axis_size("sub")
    pairs = [[2 * g, 2 * g + 1] for g in range(sections // 2)]
    alike = [[2 * g + p for g in range(sections // 2)] for p in range(2)]
    flat = jnp.sum(lax.all_gather(flat, "sec", axis_index_groups=pairs), axis=0)
    spread = jnp.broadcast_to(flat[None], (sections // 2, *flat.shape))
    flat = jnp.sum(lax.all_to_all(spread, "sec", 0, 0, axis_index_groups=alike, tiled=True), axis=0)
    spread = jnp.broadcast_to(flat[None], (subs, *flat.shape))
    flat = jnp.sum(lax.all_to_all(spread, "sub", 0, 0, tiled=True), axis=0)
    return flat.reshape(shape)


def split(value):
    high = value.astype(jnp.bfloat16)
    return high, (value - high.astype(jnp.float32)).astype(jnp.bfloat16)


def rows_split(value):
    return jnp.concatenate(split(value), axis=0)


def columns_split(value):
    return jnp.concatenate(split(value), axis=1)


def product(rows, columns):
    all_four = jnp.dot(rows, columns, preferred_element_type=jnp.float32)
    half, width = all_four.shape[0] // 2, all_four.shape[1] // 2
    top = all_four[:half, :width] + (all_four[:half, width:] + all_four[half:, :width])
    return top + all_four[half:, width:]


def prepare_kernel(odd, side, coupling_in, pair_in, residual_in, basis_in, inverse_in, sweep, tiles, start, near, far, sides, basis_rows, basis_columns, coarse_rows, coupling, pair, residual, basis, inverse_rows, sems):
    blocks, nodes, columns = residual.shape
    loads = [
        pltpu.make_async_copy(source, target, sems.at[i])
        for i, (source, target) in enumerate(
            (
                (pair_in, pair),
                (coupling_in, coupling),
                (residual_in, residual),
                (inverse_in, inverse_rows),
                (basis_in, basis),
            )
        )
    ]
    for load in loads:
        load.start()
    for load in loads[:3]:
        load.wait()
    row = lax.broadcasted_iota(jnp.int32, (nodes, nodes), 0)
    own = (row == lax.broadcasted_iota(jnp.int32, (nodes, nodes), 1)).astype(jnp.float32)
    for b in range(blocks):
        inverse = pair[b][:, nodes:]
        direct = pair[b][:, :nodes]
        start[b] = dot(inverse, residual[b])
        beside = -dot(inverse, coupling[b])
        centre = own - dot(inverse, direct)
        high, low = split(beside)
        sweep[b, :nodes, : 2 * nodes] = high
        sweep[b, nodes:, : 2 * nodes] = low
        high, low = split(centre)
        sweep[b, :nodes, 2 * nodes :] = high
        sweep[b, nodes:, 2 * nodes :] = low
        high, low = split(coupling[b])
        tiles[b, :nodes, : 2 * nodes] = high
        tiles[b, nodes:, : 2 * nodes] = low
        high, low = split(direct)
        tiles[b, :nodes, 2 * nodes :] = high
        tiles[b, nodes:, 2 * nodes :] = low
        if b == 0:
            to_previous = jnp.concatenate([beside[:, :nodes], centre], axis=1)
        if b == blocks - 1:
            to_next = jnp.concatenate([beside[:, nodes:], centre], axis=1)
        sides[b] = jnp.broadcast_to(side[b : b + 1].T, sides.shape[1:])
    even = odd[1] == 0
    near[:nodes] = jnp.where(even, start[blocks - 1], start[0])
    far[:nodes] = jnp.where(even, start[0], start[blocks - 1])
    near[nodes:] = jnp.where(even, to_next, to_previous)
    far[nodes:] = jnp.where(even, to_previous, to_next)
    for load in loads[3:]:
        load.wait()
    coarse_rows[...] = rows_split(inverse_rows[...])
    parts = rows_split(basis[...])
    basis_rows[...] = parts
    basis_columns[...] = parts.astype(jnp.float32).T.astype(jnp.bfloat16)


def first_sweep_kernel(tiles, start, out):
    blocks, nodes, _ = start.shape
    parts = [columns_split(start[b]) for b in range(blocks)]
    nothing = jnp.zeros_like(parts[0])
    for b in range(blocks):
        before = parts[b - 1] if b else nothing
        after = parts[b + 1] if b + 1 < blocks else nothing
        out[b] = start[b] + product(tiles[b], jnp.concatenate([before, after, parts[b]], axis=0))


def sweep_kernel(odd, tiles, start, partial, near, far, near_tile, far_tile, out, one, two):
    blocks, nodes, _ = start.shape
    even = odd[1] == 0
    low = jnp.where(even, far[:nodes], near[:nodes])
    high = jnp.where(even, near[:nodes], far[:nodes])
    low_tile = rows_split(jnp.where(even, far_tile[nodes:], near_tile[nodes:]))
    high_tile = rows_split(jnp.where(even, near_tile[nodes:], far_tile[nodes:]))
    low_parts, high_parts = columns_split(low), columns_split(high)
    first, last = columns_split(start[0]), columns_split(start[blocks - 1])
    one[0] = columns_split(low + product(low_tile, jnp.concatenate([first, low_parts], axis=0)))
    one[blocks + 1] = columns_split(high + product(high_tile, jnp.concatenate([last, high_parts], axis=0)))
    one[1] = columns_split(partial[0] + product(tiles[0][:, :nodes], low_parts))
    one[blocks] = columns_split(partial[blocks - 1] + product(tiles[blocks - 1][:, nodes : 2 * nodes], high_parts))
    for b in range(1, blocks - 1):
        one[b + 1] = columns_split(partial[b])
    source, target = one, two
    for sweep in range(1, SWEEPS - 1):
        final = sweep == SWEEPS - 2
        for b in range(blocks):
            near_by = jnp.concatenate([source[b], source[b + 2], source[b + 1]], axis=0)
            new = start[b] + product(tiles[b], near_by)
            if final:
                out[b] = new
            else:
                target[b + 1] = columns_split(new)
        if not final:
            target[0] = columns_split(low + product(low_tile, jnp.concatenate([source[1], source[0]], axis=0)))
            target[blocks + 1] = columns_split(
                high + product(high_tile, jnp.concatenate([source[blocks], source[blocks + 1]], axis=0))
            )
        source, target = target, source


def update_kernel(odd, coarse_rows, gathered, basis_columns, local, update, near_face, far_face, near_block, far_block):
    blocks, nodes, _ = local.shape
    faces = near_face.shape[1]
    correction = columns_split(product(coarse_rows[...], columns_split(gathered[...])))
    width = correction.shape[1] // 2
    correction = jnp.concatenate([correction, correction], axis=0)
    for b in range(blocks):
        both = jnp.dot(
            basis_columns[b * nodes : (b + 1) * nodes], correction, preferred_element_type=jnp.float32
        )
        new = local[b] + (both[:, :width] + both[:, width:])
        update[b] = new
        south, north = new[:faces], new[nodes - faces :]
        even = odd[0] == 0
        near_face[b] = jnp.where(even, north, south)
        far_face[b] = jnp.where(even, south, north)
    even = odd[1] == 0
    near_block[...] = jnp.where(even, update[blocks - 1], update[0])
    far_block[...] = jnp.where(even, update[0], update[blocks - 1])


def image_blocks(odd, tiles, sides, update, near_face, far_face, near_block, far_block):
    blocks, nodes, _ = update.shape
    faces = near_face.shape[1]
    even = odd[1] == 0
    low = jnp.where(even, far_block[...], near_block[...])
    high = jnp.where(even, near_block[...], far_block[...])
    parts = [columns_split(value) for value in (low, *(update[b] for b in range(blocks)), high)]
    even = odd[0] == 0
    for b in range(blocks):
        linear = product(tiles[b], jnp.concatenate([parts[b], parts[b + 2], parts[b + 1]], axis=0))
        below = jnp.where(even, far_face[b], near_face[b])
        above = jnp.where(even, near_face[b], far_face[b])
        yield b, jnp.concatenate(
            [
                linear[:faces] + sides[b, :faces] * below,
                linear[faces : nodes - faces],
                linear[nodes - faces :] + sides[b, faces:] * above,
            ],
            axis=0,
        )


def send_out(projected, spread, sems):
    copies = [
        pltpu.make_async_copy(projected, spread.at[i], sems.at[i]) for i in range(spread.shape[0])
    ]
    for copy in copies:
        copy.start()
    return copies


def image_kernel(odd, tiles, sides, basis_rows, pair, residual, update, far_face, near_face, far_block, near_block, image_out, rest_out, spread, start, near, far, image, rest, flat, projected, sems, stores):
    blocks, nodes, _ = update.shape
    for b, new in image_blocks(odd, tiles, sides, update, near_face, far_face, near_block, far_block):
        image[b] = new
        left = residual[b] - new
        rest[b] = left
        flat[b * nodes : (b + 1) * nodes] = columns_split(left)
    projected[...] = product(basis_rows[...], flat[...])
    copies = send_out(projected, spread, sems)
    for i, (source, target) in enumerate(((image, image_out), (rest, rest_out))):
        copies.append(pltpu.make_async_copy(source, target, stores.at[i]))
        copies[-1].start()
    for b in range(blocks):
        start[b] = product(rows_split(pair[b][:, nodes:]), flat[b * nodes : (b + 1) * nodes])
    even = odd[1] == 0
    near[...] = jnp.where(even, start[blocks - 1], start[0])
    far[...] = jnp.where(even, start[0], start[blocks - 1])
    for copy in copies:
        copy.wait()


def project_kernel(basis, field, spread, projected, sems):
    blocks, nodes, columns = field.shape
    projected[...] = dot(basis[...], field[...].reshape(blocks * nodes, columns))
    for copy in send_out(projected, spread, sems):
        copy.wait()


def sums_kernel(odd, tiles, sides, image, rest, update, far_face, near_face, far_block, near_block, sums):
    nodes, columns = update.shape[1:]
    parts = [jnp.zeros((8, columns), jnp.float32) for _ in range(5)]

    def inner(left, right):
        return jnp.sum((left * right).reshape(nodes // 8, 8, columns), axis=0)

    for b, new in image_blocks(odd, tiles, sides, update, near_face, far_face, near_block, far_block):
        change = new * SCALE
        left, right = image[b], rest[b]
        for i, (x, y) in enumerate(((left, right), (left, left), (change, right), (change, left), (change, change))):
            parts[i] = parts[i] + inner(x, y)
    for i in range(5):
        sums[i : i + 1] = jnp.sum(parts[i], axis=0, keepdims=True)


def call(kernel, outs, scratch, *operands, slow=0):
    spaces = [pltpu.VMEM] * (len(operands) - slow) + [pltpu.HBM] * slow
    spaces = [pltpu.SMEM if operand.dtype == jnp.int32 else space for operand, space in zip(operands, spaces)]
    return pl.pallas_call(
        kernel,
        out_shape=[space(shape, kind) for shape, kind, space in outs],
        in_specs=[pl.BlockSpec(memory_space=space) for space in spaces],
        out_specs=[pl.BlockSpec(memory_space=space) for _, _, space in outs],
        scratch_shapes=scratch,
        compiler_params=pltpu.CompilerParams(vmem_limit_bytes=12 << 20),
        cost_estimate=pl.CostEstimate(flops=1000, transcendentals=0, bytes_accessed=1000),
    )(
        *(
            operand if space is pltpu.SMEM else pltpu.with_memory_space_constraint(operand, space)
            for operand, space in zip(operands, spaces)
        )
    )


def shards(forcing, coupling, diag_pair, side, basis, coarse_inverse):
    residual = forcing[0]
    basis_all = basis[0]
    blocks, nodes, columns = residual.shape
    faces = side.shape[2] // 2
    coarse, own_coarse = coarse_inverse.shape[2], coarse_inverse.shape[1]
    odd = jnp.stack([lax.axis_index("sec") % 2, lax.axis_index("sub") % 2]).astype(jnp.int32)
    wide, thin, fast = jnp.float32, jnp.bfloat16, pltpu.VMEM
    subs = lax.axis_size("sub")
    block = ((nodes, columns), wide, fast)
    field = ((blocks, nodes, columns), wide, fast)
    kept = ((blocks, nodes, columns), wide, pltpu.HBM)
    face = ((blocks, faces, columns), wide, fast)
    tile = ((blocks, 2 * nodes, 3 * nodes), thin, fast)
    padded = pltpu.VMEM((blocks + 2, nodes, 2 * columns), thin)
    spread_out = ((subs, own_coarse, columns), wide, pltpu.HBM)
    spreading = [pltpu.VMEM((own_coarse, columns), wide), pltpu.SemaphoreType.DMA((subs,))]

    (spread,) = call(project_kernel, [spread_out], spreading, basis_all, residual)
    spread, odd, residual, coupling, diag_pair, side, basis_all = lax.optimization_barrier(
        (spread, odd, residual, coupling, diag_pair, side, basis_all)
    )
    pair = diag_pair[0]
    sweep, tiles, start, near, far, sides, basis_rows, basis_columns, coarse_rows = call(
        prepare_kernel,
        [
            tile,
            tile,
            field,
            ((2 * nodes, columns), wide, fast),
            ((2 * nodes, columns), wide, fast),
            ((blocks, 2 * faces, columns), wide, fast),
            ((2 * own_coarse, blocks * nodes), thin, fast),
            ((blocks * nodes, 2 * own_coarse), thin, fast),
            ((2 * own_coarse, coarse), thin, fast),
        ],
        [
            pltpu.VMEM((blocks, nodes, columns), wide),
            pltpu.VMEM((blocks, nodes, columns), wide),
            pltpu.VMEM((blocks, nodes, columns), wide),
            pltpu.VMEM(basis_all.shape, wide),
            pltpu.VMEM((own_coarse, coarse), wide),
            pltpu.SemaphoreType.DMA((5,)),
        ],
        odd, side[0], coupling[0], pair, residual, basis_all, coarse_inverse[0],
        slow=5,
    )

    def precondition(start, near, far, near_tile, far_tile, spread):
        gathered = gather_sub(spread)
        (partial,) = call(first_sweep_kernel, [field], [], sweep, start)
        (local,) = call(sweep_kernel, [field], [padded] * 2, odd, sweep, start, partial, near, far, near_tile, far_tile)
        update, near_face, far_face, near_block, far_block = call(
            update_kernel, [field, face, face, block, block], [], odd, coarse_rows, gathered, basis_columns, local
        )
        faces_in = swap(near_face, far_face, "sec")
        blocks_in = swap(near_block, far_block, "sub")
        return update, *faces_in[::-1], *blocks_in[::-1]

    halo = swap(near, far, "sub")
    first, *given = precondition(start, *halo, *halo, spread)
    image, rest, spread, start, near, far = call(
        image_kernel,
        [kept, kept, spread_out, field, block, block],
        [
            pltpu.VMEM((blocks, nodes, columns), wide),
            pltpu.VMEM((blocks, nodes, columns), wide),
            pltpu.VMEM((blocks * nodes, 2 * columns), thin),
            *spreading,
            pltpu.SemaphoreType.DMA((2,)),
        ],
        odd, tiles, sides, basis_rows, pair, residual, first, *given,
    )
    second, *given = precondition(start, *swap(near, far, "sub"), *halo, spread)
    (sums,) = call(sums_kernel, [((5, columns), wide, fast)], [], odd, tiles, sides, image, rest, second, *given)
    sums = total(sums)
    short = -sums[0] / sums[1]
    step = 1.0 - short
    upper = step * (sums[2] + short * sums[3])
    scaled = step / SCALE
    lower = short * short * sums[1] + 2.0 * short * scaled * sums[3] + scaled * scaled * sums[4]
    step_next = upper / SCALE / lower
    result = (step + step_next * short) * first + (step_next * step) * second
    return result[None]


def solution(mesh):
    placed = (
        P("sec", "sub", None, None),
        P("sec", "sub", None, None),
        P("sec", "sub", None, None),
        P("sec", "sub", None),
        P("sec", "sub", None),
        P("sec", "sub", None),
    )
    return jax.shard_map(
        shards, mesh=mesh, in_specs=placed, out_specs=P("sec", "sub", None, None), check_vma=False
    )
```

```python
import jax
import jax.numpy as jnp
from jax import lax
from jax.experimental import pallas as pl
from jax.experimental.pallas import tpu as pltpu
from jax.sharding import PartitionSpec as P

SWEEPS = 4
SCALE = 2.0**-16

PRECISE = lax.Precision.HIGHEST


def dot(left, right):
    return jnp.dot(left, right, precision=PRECISE, preferred_element_type=jnp.float32)


def pairings(axis):
    count = lax.axis_size(axis)
    near = [(i, i ^ 1) for i in range(count)]
    low = [(i, i + 1) for i in range(1, count - 1, 2)]
    return near, low + [(target, source) for source, target in low]


def swap(to_near, to_far, axis):
    near, far = pairings(axis)
    from_far = lax.ppermute(to_far, axis, far)
    return lax.ppermute(to_near, axis, near), from_far


def gather_sub(spread):
    return lax.all_to_all(spread, "sub", 0, 0, tiled=True).reshape(-1, *spread.shape[2:])


def total(sums):
    sections, subs = lax.axis_size("sec"), lax.axis_size("sub")
    planes = sections // 4
    within = [
        [(4 * p + 2 * run + core) * subs + sub for run in range(2) for sub in range(subs)]
        for p in range(planes)
        for core in range(2)
    ]
    across = [[4 * p + 2 * run + core for p in range(planes) for core in range(2)] for run in range(2)]
    flat = sums.reshape(1, -1)
    for axes, groups in ((("sec", "sub"), within), ("sec", across)):
        spread = jnp.broadcast_to(flat[None], (len(groups[0]), *flat.shape))
        flat = jnp.sum(lax.all_to_all(spread, axes, 0, 0, axis_index_groups=groups, tiled=True), axis=0)
    return flat.reshape(sums.shape)


def split(value):
    high = value.astype(jnp.bfloat16)
    return high, (value - high.astype(jnp.float32)).astype(jnp.bfloat16)


def rows_split(value):
    return jnp.concatenate(split(value), axis=0)


def columns_split(value):
    return jnp.concatenate(split(value), axis=1)


def product(rows, columns):
    all_four = jnp.dot(rows, columns, preferred_element_type=jnp.float32)
    half, width = all_four.shape[0] // 2, all_four.shape[1] // 2
    top = all_four[:half, :width] + (all_four[:half, width:] + all_four[half:, :width])
    return top + all_four[half:, width:]


def pair_split(value):
    high, low = split(value)
    both = jnp.concatenate([high.astype(jnp.float32), low.astype(jnp.float32)], axis=1)
    return both.astype(jnp.bfloat16)


def pair_product(pairs, columns):
    both = jnp.dot(pairs, jnp.concatenate([columns, columns], axis=0), preferred_element_type=jnp.float32)
    width = both.shape[1] // 2
    return both[:, :width] + both[:, width:]


def tile_product(beside, centre, before, after, own):
    return product(beside, jnp.concatenate([before, after], axis=0)) + pair_product(centre, own)


def block_sweep(pair, coupling, field):
    nodes = pair.shape[0]
    inverse = rows_split(pair[:, nodes:])
    row = lax.broadcasted_iota(jnp.int32, (nodes, nodes), 0)
    unit = (row == lax.broadcasted_iota(jnp.int32, (nodes, nodes), 1)).astype(jnp.float32)
    beside = -product(inverse, columns_split(coupling))
    own = unit - product(inverse, columns_split(pair))[:, :nodes]
    return product(inverse, columns_split(field)), beside, own


def start_all(pairs, sems):
    loads = [pltpu.make_async_copy(source, target, sems.at[i]) for i, (source, target) in enumerate(pairs)]
    for load in loads:
        load.start()
    return loads


def edge_kernel(odd, coupling_in, pair_in, residual_in, near, far, coupling, pair, residual, sems):
    blocks, nodes = pair_in.shape[:2]
    loads = start_all(
        [
            (source.at[b], target.at[i])
            for source, target in ((pair_in, pair), (coupling_in, coupling), (residual_in, residual))
            for i, b in enumerate((0, blocks - 1))
        ],
        sems,
    )
    for load in loads:
        load.wait()
    even = odd[1] == 0
    start, beside, own = block_sweep(pair[0], coupling[0], residual[0])
    last, beyond, own_last = block_sweep(pair[1], coupling[1], residual[1])
    to_previous = jnp.concatenate([beside[:, :nodes], own], axis=1)
    to_next = jnp.concatenate([beyond[:, nodes:], own_last], axis=1)
    near[:nodes] = jnp.where(even, last, start)
    far[:nodes] = jnp.where(even, start, last)
    near[nodes:] = jnp.where(even, to_next, to_previous)
    far[nodes:] = jnp.where(even, to_previous, to_next)


def prepare_kernel(side, coupling_in, pair_in, residual_in, basis_in, inverse_in, sweep, sweep_own, tiles_out, tiles_own_out, start, sides_out, basis_rows_out, basis_columns, coarse_rows, coupling, pair, residual, basis, inverse_rows, tiles, tiles_own, sides, basis_rows, sems, stores):
    blocks, nodes, columns = residual.shape
    loads = start_all(
        [
            (pair_in, pair),
            (coupling_in, coupling),
            (residual_in, residual),
            (inverse_in, inverse_rows),
            (basis_in, basis),
        ],
        sems,
    )
    for load in loads[:3]:
        load.wait()
    for b in range(blocks):
        start[b], beside, own = block_sweep(pair[b], coupling[b], residual[b])
        sweep[b] = rows_split(beside)
        sweep_own[b] = pair_split(own)
        tiles[b] = rows_split(coupling[b])
        tiles_own[b] = pair_split(pair[b][:, :nodes])
        sides[b] = jnp.broadcast_to(side[b : b + 1].T, sides.shape[1:])
    for load in loads[3:]:
        load.wait()
    parts = rows_split(basis[...])
    basis_rows[...] = parts
    copies = start_all(
        [(tiles, tiles_out), (tiles_own, tiles_own_out), (sides, sides_out), (basis_rows, basis_rows_out)], stores
    )
    coarse_rows[...] = rows_split(inverse_rows[...])
    basis_columns[...] = parts.astype(jnp.float32).T.astype(jnp.bfloat16)
    for copy in copies:
        copy.wait()


def first_sweep_kernel(tiles, tiles_own, start, out):
    blocks, nodes, _ = start.shape
    parts = [columns_split(start[b]) for b in range(blocks)]
    nothing = jnp.zeros_like(parts[0])
    for b in range(blocks):
        before = parts[b - 1] if b else nothing
        after = parts[b + 1] if b + 1 < blocks else nothing
        out[b] = start[b] + tile_product(tiles[b], tiles_own[b], before, after, parts[b])


def sweep_kernel(odd, tiles, tiles_own, start, partial, far, near, far_tile, near_tile, out, one, two):
    blocks, nodes, _ = start.shape
    even = odd[1] == 0
    low = jnp.where(even, far[...], near[...])
    high = jnp.where(even, near[...], far[...])
    low_tile = rows_split(jnp.where(even, far_tile[...], near_tile[...]))
    high_tile = rows_split(jnp.where(even, near_tile[...], far_tile[...]))
    low_parts, high_parts = columns_split(low), columns_split(high)
    first, last = columns_split(start[0]), columns_split(start[blocks - 1])
    one[0] = columns_split(low + product(low_tile, jnp.concatenate([first, low_parts], axis=0)))
    one[blocks + 1] = columns_split(high + product(high_tile, jnp.concatenate([last, high_parts], axis=0)))
    one[1] = columns_split(partial[0] + product(tiles[0][:, :nodes], low_parts))
    one[blocks] = columns_split(partial[blocks - 1] + product(tiles[blocks - 1][:, nodes : 2 * nodes], high_parts))
    for b in range(1, blocks - 1):
        one[b + 1] = columns_split(partial[b])
    source, target = one, two
    for sweep in range(1, SWEEPS - 1):
        final = sweep == SWEEPS - 2
        for b in range(blocks):
            new = start[b] + tile_product(tiles[b], tiles_own[b], source[b], source[b + 2], source[b + 1])
            if final:
                out[b] = new
            else:
                target[b + 1] = columns_split(new)
        if not final:
            target[0] = columns_split(low + product(low_tile, jnp.concatenate([source[1], source[0]], axis=0)))
            target[blocks + 1] = columns_split(
                high + product(high_tile, jnp.concatenate([source[blocks], source[blocks + 1]], axis=0))
            )
        source, target = target, source


def keeping_sweep_kernel(odd, tiles, tiles_own, start, partial, far, near, out, far_kept, near_kept, one, two, sems):
    nodes = start.shape[1]
    far_tile, near_tile = far.at[nodes : 2 * nodes], near.at[nodes : 2 * nodes]
    copies = start_all([(far_tile, far_kept), (near_tile, near_kept)], sems)
    sweep_kernel(
        odd, tiles, tiles_own, start, partial, far.at[:nodes], near.at[:nodes], far_tile, near_tile, out, one, two
    )
    for copy in copies:
        copy.wait()


def update_kernel(odd, coarse_rows, gathered, basis_columns, local, update, near_face, far_face, near_block, far_block):
    blocks, nodes, _ = local.shape
    faces = near_face.shape[1]
    correction = columns_split(product(coarse_rows[...], columns_split(gathered[...])))
    for b in range(blocks):
        new = local[b] + pair_product(basis_columns[b * nodes : (b + 1) * nodes], correction)
        update[b] = new
        south, north = new[:faces], new[nodes - faces :]
        even = odd[0] == 0
        near_face[b] = jnp.where(even, north, south)
        far_face[b] = jnp.where(even, south, north)
    even = odd[1] == 0
    near_block[...] = jnp.where(even, update[blocks - 1], update[0])
    far_block[...] = jnp.where(even, update[0], update[blocks - 1])


def image_blocks(odd, tiles, tiles_own, sides, update, near_face, far_face, near_block, far_block):
    blocks, nodes, _ = update.shape
    faces = near_face.shape[1]
    even = odd[1] == 0
    low = jnp.where(even, far_block[...], near_block[...])
    high = jnp.where(even, near_block[...], far_block[...])
    parts = [columns_split(value) for value in (low, *(update[b] for b in range(blocks)), high)]
    even = odd[0] == 0
    for b in range(blocks):
        linear = tile_product(tiles[b], tiles_own[b], parts[b], parts[b + 2], parts[b + 1])
        below = jnp.where(even, far_face[b], near_face[b])
        above = jnp.where(even, near_face[b], far_face[b])
        yield b, jnp.concatenate(
            [
                linear[:faces] + sides[b, :faces] * below,
                linear[faces : nodes - faces],
                linear[nodes - faces :] + sides[b, faces:] * above,
            ],
            axis=0,
        )


def send_out(projected, spread, sems):
    return start_all([(projected, spread.at[i]) for i in range(spread.shape[0])], sems)


def image_kernel(odd, tiles, tiles_own, sides, basis_rows, pair, residual, update, near_face, near_block, far_block, far_face, image_out, rest_out, spread, start, near, far, image, rest, flat, projected, edges, sems, stores):
    blocks, nodes, _ = update.shape
    for b, new in image_blocks(odd, tiles, tiles_own, sides, update, near_face, far_face, near_block, far_block):
        image[b] = new
        left = residual[b] - new
        rest[b] = left
        flat[b * nodes : (b + 1) * nodes] = columns_split(left)
    projected[...] = product(basis_rows[...], flat[...])
    copies = send_out(projected, spread, sems)
    for b in (0, blocks - 1, *range(1, blocks - 1)):
        start[b] = product(rows_split(pair[b][:, nodes:]), flat[b * nodes : (b + 1) * nodes])
        if b == blocks - 1:
            even = odd[1] == 0
            edges[0] = jnp.where(even, start[blocks - 1], start[0])
            edges[1] = jnp.where(even, start[0], start[blocks - 1])
            copies += start_all(
                [(edges.at[0], near), (edges.at[1], far), (image, image_out), (rest, rest_out)], stores
            )
    for copy in copies:
        copy.wait()


def project_kernel(basis_in, field_in, spread, basis, field, projected, sems, arrived):
    blocks, nodes, columns = field.shape
    for load in start_all([(basis_in, basis), (field_in, field)], arrived):
        load.wait()
    projected[...] = dot(basis[...], field[...].reshape(blocks * nodes, columns))
    for copy in send_out(projected, spread, sems):
        copy.wait()


def sums_kernel(odd, tiles, tiles_own, sides, image, rest, update, near_face, near_block, far_block, far_face, sums):
    nodes, columns = update.shape[1:]
    parts = [jnp.zeros((8, columns), jnp.float32) for _ in range(5)]

    def inner(left, right):
        return jnp.sum((left * right).reshape(nodes // 8, 8, columns), axis=0)

    for b, new in image_blocks(odd, tiles, tiles_own, sides, update, near_face, far_face, near_block, far_block):
        change = new * SCALE
        left, right = image[b], rest[b]
        for i, (x, y) in enumerate(((left, right), (left, left), (change, right), (change, left), (change, change))):
            parts[i] = parts[i] + inner(x, y)
    for i in range(5):
        sums[i : i + 1] = jnp.sum(parts[i], axis=0, keepdims=True)


def call(kernel, outs, scratch, *operands, slow=0):
    specs, given = [], []
    for at, operand in enumerate(operands):
        space = pltpu.HBM if at >= len(operands) - slow else pltpu.VMEM
        if operand.dtype == jnp.int32:
            space = pltpu.SMEM
        elif operand.size > 2 * operand.shape[-1] ** 2 or space is pltpu.HBM:
            operand = pltpu.with_memory_space_constraint(operand, space)
        specs.append(pl.BlockSpec(memory_space=space))
        given.append(operand)
    return pl.pallas_call(
        kernel,
        out_shape=[(space or jax.ShapeDtypeStruct)(shape, kind) for shape, kind, space in outs],
        in_specs=specs,
        out_specs=[pl.BlockSpec(memory_space=space or pltpu.VMEM) for _, _, space in outs],
        scratch_shapes=scratch,
        compiler_params=pltpu.CompilerParams(vmem_limit_bytes=12 << 20),
        cost_estimate=pl.CostEstimate(flops=1000, transcendentals=0, bytes_accessed=1000),
    )(*given)


def shards(forcing, coupling, diag_pair, side, basis, coarse_inverse):
    residual = forcing[0]
    basis_all = basis[0]
    blocks, nodes, columns = residual.shape
    faces = side.shape[2] // 2
    coarse, own_coarse = coarse_inverse.shape[2], coarse_inverse.shape[1]
    odd = jnp.stack([lax.axis_index("sec") % 2, lax.axis_index("sub") % 2]).astype(jnp.int32)
    wide, thin, fast = jnp.float32, jnp.bfloat16, pltpu.VMEM
    subs = lax.axis_size("sub")
    block = ((nodes, columns), wide, None)
    edge = ((nodes, columns), wide, pltpu.HBM)
    small = ((2 * nodes, columns), wide, None)
    field = ((blocks, nodes, columns), wide, fast)
    kept = ((blocks, nodes, columns), wide, pltpu.HBM)
    face = ((blocks, faces, columns), wide, fast)
    tile = ((blocks, 2 * nodes, 2 * nodes), thin)
    tile_own = ((blocks, nodes, 2 * nodes), thin)
    padded = pltpu.VMEM((blocks + 2, nodes, 2 * columns), thin)
    spread_out = ((subs, own_coarse, columns), wide, pltpu.HBM)
    spreading = [pltpu.VMEM((own_coarse, columns), wide), pltpu.SemaphoreType.DMA((subs,))]

    (spread,) = call(
        project_kernel,
        [spread_out],
        [
            pltpu.VMEM(basis_all.shape, wide),
            pltpu.VMEM((blocks, nodes, columns), wide),
            *spreading,
            pltpu.SemaphoreType.DMA((2,)),
        ],
        basis_all, residual,
        slow=2,
    )
    spread, odd, residual, coupling, diag_pair, side, basis_all = lax.optimization_barrier(
        (spread, odd, residual, coupling, diag_pair, side, basis_all)
    )
    pair = diag_pair[0]
    near, far = call(
        edge_kernel,
        [small, small],
        [pltpu.VMEM((2, nodes, columns), wide)] * 3 + [pltpu.SemaphoreType.DMA((6,))],
        odd, coupling[0], pair, residual,
        slow=3,
    )
    halo = swap(near, far, "sub")
    sweep, sweep_own, tiles, tiles_own, start, sides, basis_rows, basis_columns, coarse_rows = call(
        prepare_kernel,
        [
            (*tile, fast),
            (*tile_own, fast),
            (*tile, pltpu.HBM),
            (*tile_own, pltpu.HBM),
            field,
            ((blocks, 2 * faces, columns), wide, pltpu.HBM),
            ((2 * own_coarse, blocks * nodes), thin, pltpu.HBM),
            ((blocks * nodes, 2 * own_coarse), thin, fast),
            ((2 * own_coarse, coarse), thin, fast),
        ],
        [
            pltpu.VMEM((blocks, nodes, columns), wide),
            pltpu.VMEM((blocks, nodes, columns), wide),
            pltpu.VMEM((blocks, nodes, columns), wide),
            pltpu.VMEM(basis_all.shape, wide),
            pltpu.VMEM((own_coarse, coarse), wide),
            pltpu.VMEM(*tile),
            pltpu.VMEM(*tile_own),
            pltpu.VMEM((blocks, 2 * faces, columns), wide),
            pltpu.VMEM((2 * own_coarse, blocks * nodes), thin),
            pltpu.SemaphoreType.DMA((5,)),
            pltpu.SemaphoreType.DMA((4,)),
        ],
        side[0], coupling[0], pair, residual, basis_all, coarse_inverse[0],
        slow=5,
    )

    def precondition(start, near, far, kept, spread):
        gathered = gather_sub(spread)
        (partial,) = call(first_sweep_kernel, [field], [], sweep, sweep_own, start)
        given = (odd, sweep, sweep_own, start, partial, far, near)
        if kept:
            (local,) = call(sweep_kernel, [field], [padded] * 2, *given, *kept)
        else:
            local, *kept = call(
                keeping_sweep_kernel,
                [field, edge, edge],
                [padded, padded, pltpu.SemaphoreType.DMA((2,))],
                *given,
            )
        update, near_face, far_face, near_block, far_block = call(
            update_kernel, [field, face, face, block, block], [], odd, coarse_rows, gathered, basis_columns, local
        )
        faces_in = swap(near_face, far_face, "sec")
        blocks_in = swap(near_block, far_block, "sub")
        return kept, update, faces_in[0], blocks_in[0], blocks_in[1], faces_in[1]

    kept_tiles, first, *given = precondition(start, *halo, None, spread)
    image, rest, spread, start, near, far = call(
        image_kernel,
        [kept, kept, spread_out, field, edge, edge],
        [
            pltpu.VMEM((blocks, nodes, columns), wide),
            pltpu.VMEM((blocks, nodes, columns), wide),
            pltpu.VMEM((blocks * nodes, 2 * columns), thin),
            pltpu.VMEM((own_coarse, columns), wide),
            pltpu.VMEM((2, nodes, columns), wide),
            pltpu.SemaphoreType.DMA((subs,)),
            pltpu.SemaphoreType.DMA((4,)),
        ],
        odd, tiles, tiles_own, sides, basis_rows, pair, residual, first, *given,
    )
    _, second, *given = precondition(start, *swap(near, far, "sub"), kept_tiles, spread)
    (sums,) = call(sums_kernel, [((5, columns), wide, fast)], [], odd, tiles, tiles_own, sides, image, rest, second, *given)
    sums = total(sums)
    short = -sums[0] / sums[1]
    step = 1.0 - short
    upper = step * (sums[2] + short * sums[3])
    scaled = step / SCALE
    lower = short * short * sums[1] + 2.0 * short * scaled * sums[3] + scaled * scaled * sums[4]
    step_next = upper / SCALE / lower
    result = (step + step_next * short) * first + (step_next * step) * second
    return result[None]


def solution(mesh):
    placed = (
        P("sec", "sub", None, None),
        P("sec", "sub", None, None),
        P("sec", "sub", None, None),
        P("sec", "sub", None),
        P("sec", "sub", None),
        P("sec", "sub", None),
    )
    return jax.shard_map(
        shards, mesh=mesh, in_specs=placed, out_specs=P("sec", "sub", None, None), check_vma=False
    )
```

```python
import jax
import jax.numpy as jnp
from jax import lax
from jax.experimental import pallas as pl
from jax.experimental.pallas import tpu as pltpu
from jax.sharding import PartitionSpec as P

SWEEPS = 4
SCALE = 2.0**-16

PRECISE = lax.Precision.HIGHEST


def dot(left, right):
    return jnp.dot(left, right, precision=PRECISE, preferred_element_type=jnp.float32)


def pairings(axis):
    count = lax.axis_size(axis)
    near = [(i, i ^ 1) for i in range(count)]
    low = [(i, i + 1) for i in range(1, count - 1, 2)]
    return near, low + [(target, source) for source, target in low]


def swap(to_near, to_far, axis):
    near, far = pairings(axis)
    from_far = lax.ppermute(to_far, axis, far)
    return lax.ppermute(to_near, axis, near), from_far


def gather_sub(spread):
    return lax.all_to_all(spread, "sub", 0, 0, tiled=True).reshape(-1, *spread.shape[2:])


def total(sums):
    sections, subs = lax.axis_size("sec"), lax.axis_size("sub")
    planes = sections // 4
    within = [
        [(4 * p + 2 * run + core) * subs + sub for run in range(2) for sub in range(subs)]
        for p in range(planes)
        for core in range(2)
    ]
    across = [[4 * p + 2 * run + core for p in range(planes) for core in range(2)] for run in range(2)]
    flat = sums.reshape(1, -1)
    for axes, groups in ((("sec", "sub"), within), ("sec", across)):
        spread = jnp.broadcast_to(flat[None], (len(groups[0]), *flat.shape))
        flat = jnp.sum(lax.all_to_all(spread, axes, 0, 0, axis_index_groups=groups, tiled=True), axis=0)
    return flat.reshape(sums.shape)


def split(value):
    high = value.astype(jnp.bfloat16)
    return high, (value - high.astype(jnp.float32)).astype(jnp.bfloat16)


def rows_split(value):
    return jnp.concatenate(split(value), axis=0)


def columns_split(value):
    return jnp.concatenate(split(value), axis=1)


def product(rows, columns):
    all_four = jnp.dot(rows, columns, preferred_element_type=jnp.float32)
    half, width = all_four.shape[0] // 2, all_four.shape[1] // 2
    top = all_four[:half, :width] + (all_four[:half, width:] + all_four[half:, :width])
    return top + all_four[half:, width:]


def pair_split(value):
    high, low = split(value)
    both = jnp.concatenate([high.astype(jnp.float32), low.astype(jnp.float32)], axis=1)
    return both.astype(jnp.bfloat16)


def pair_product(pairs, columns):
    both = jnp.dot(pairs, jnp.concatenate([columns, columns], axis=0), preferred_element_type=jnp.float32)
    width = both.shape[1] // 2
    return both[:, :width] + both[:, width:]


def tile_product(beside, centre, before, after, own):
    return product(beside, jnp.concatenate([before, after], axis=0)) + pair_product(centre, own)


def block_sweep(pair, coupling, field):
    nodes = pair.shape[0]
    inverse = rows_split(pair[:, nodes:])
    row = lax.broadcasted_iota(jnp.int32, (nodes, nodes), 0)
    unit = (row == lax.broadcasted_iota(jnp.int32, (nodes, nodes), 1)).astype(jnp.float32)
    beside = -product(inverse, columns_split(coupling))
    own = unit - product(inverse, columns_split(pair))[:, :nodes]
    return product(inverse, columns_split(field)), beside, own


def start_all(pairs, sems):
    loads = [pltpu.make_async_copy(source, target, sems.at[i]) for i, (source, target) in enumerate(pairs)]
    for load in loads:
        load.start()
    return loads


def prepare_kernel(side, coupling_in, pair_in, residual_in, basis_in, inverse_in, sweep, sweep_own, tiles_out, tiles_own_out, edge_tiles_out, start, sides_out, basis_rows_out, basis_columns, coarse_rows, coupling, pair, residual, basis, inverse_rows, tiles, tiles_own, sides, basis_rows, sems, stores):
    blocks, nodes, columns = residual.shape
    loads = start_all(
        [
            (pair_in, pair),
            (coupling_in, coupling),
            (residual_in, residual),
            (inverse_in, inverse_rows),
            (basis_in, basis),
        ],
        sems,
    )
    for load in loads[:3]:
        load.wait()
    for b in range(blocks):
        start[b], beside, own = block_sweep(pair[b], coupling[b], residual[b])
        sweep[b] = rows_split(beside)
        sweep_own[b] = pair_split(own)
        tiles[b] = rows_split(coupling[b])
        tiles_own[b] = pair_split(pair[b][:, :nodes])
        sides[b] = jnp.broadcast_to(side[b : b + 1].T, sides.shape[1:])
    for load in loads[3:]:
        load.wait()
    parts = rows_split(basis[...])
    basis_rows[...] = parts
    copies = start_all(
        [
            (tiles, tiles_out),
            (tiles_own, tiles_own_out),
            (sides, sides_out),
            (basis_rows, basis_rows_out),
            (tiles.at[0], edge_tiles_out.at[0]),
            (tiles.at[blocks - 1], edge_tiles_out.at[1]),
        ],
        stores,
    )
    coarse_rows[...] = rows_split(inverse_rows[...])
    basis_columns[...] = parts.astype(jnp.float32).T.astype(jnp.bfloat16)
    for copy in copies:
        copy.wait()


def first_sweep_kernel(tiles, tiles_own, start, out):
    blocks, nodes, _ = start.shape
    parts = [columns_split(start[b]) for b in range(blocks)]
    nothing = jnp.zeros_like(parts[0])
    for b in range(blocks):
        before = parts[b - 1] if b else nothing
        after = parts[b + 1] if b + 1 < blocks else nothing
        out[b] = start[b] + tile_product(tiles[b], tiles_own[b], before, after, parts[b])


def sweep_kernel(odd, tiles, tiles_own, start, partial, far, near, far_tile, near_tile, out, one, two):
    blocks, nodes, _ = start.shape
    even = odd[1] == 0
    low = jnp.where(even, far[...], near[...])
    high = jnp.where(even, near[...], far[...])
    low_tile = rows_split(jnp.where(even, far_tile[...], near_tile[...]))
    high_tile = rows_split(jnp.where(even, near_tile[...], far_tile[...]))
    low_parts, high_parts = columns_split(low), columns_split(high)
    first, last = columns_split(start[0]), columns_split(start[blocks - 1])
    one[0] = columns_split(low + product(low_tile, jnp.concatenate([first, low_parts], axis=0)))
    one[blocks + 1] = columns_split(high + product(high_tile, jnp.concatenate([last, high_parts], axis=0)))
    one[1] = columns_split(partial[0] + product(tiles[0][:, :nodes], low_parts))
    one[blocks] = columns_split(partial[blocks - 1] + product(tiles[blocks - 1][:, nodes : 2 * nodes], high_parts))
    for b in range(1, blocks - 1):
        one[b + 1] = columns_split(partial[b])
    source, target = one, two
    for sweep in range(1, SWEEPS - 1):
        final = sweep == SWEEPS - 2
        for b in range(blocks):
            new = start[b] + tile_product(tiles[b], tiles_own[b], source[b], source[b + 2], source[b + 1])
            if final:
                out[b] = new
            else:
                target[b + 1] = columns_split(new)
        if not final:
            target[0] = columns_split(low + product(low_tile, jnp.concatenate([source[1], source[0]], axis=0)))
            target[blocks + 1] = columns_split(
                high + product(high_tile, jnp.concatenate([source[blocks], source[blocks + 1]], axis=0))
            )
        source, target = target, source


def keeping_sweep_kernel(odd, tiles, tiles_own, start, partial, far, near, out, far_kept, near_kept, one, two, sems):
    nodes = start.shape[1]
    far_tile, near_tile = far.at[nodes : 2 * nodes], near.at[nodes : 2 * nodes]
    copies = start_all([(far_tile, far_kept), (near_tile, near_kept)], sems)
    sweep_kernel(
        odd, tiles, tiles_own, start, partial, far.at[:nodes], near.at[:nodes], far_tile, near_tile, out, one, two
    )
    for copy in copies:
        copy.wait()


def update_kernel(odd, coarse_rows, gathered, basis_columns, local, update, near_face, far_face, near_block, far_block):
    blocks, nodes, _ = local.shape
    faces = near_face.shape[1]
    correction = columns_split(product(coarse_rows[...], columns_split(gathered[...])))
    for b in range(blocks):
        new = local[b] + pair_product(basis_columns[b * nodes : (b + 1) * nodes], correction)
        update[b] = new
        south, north = new[:faces], new[nodes - faces :]
        even = odd[0] == 0
        near_face[b] = jnp.where(even, north, south)
        far_face[b] = jnp.where(even, south, north)
    even = odd[1] == 0
    near_block[...] = jnp.where(even, update[blocks - 1], update[0])
    far_block[...] = jnp.where(even, update[0], update[blocks - 1])


def linear_kernel(tiles, tiles_own, update, out):
    blocks = update.shape[0]
    parts = [columns_split(update[b]) for b in range(blocks)]
    nothing = jnp.zeros_like(parts[0])
    for b in range(blocks):
        before = parts[b - 1] if b else nothing
        after = parts[b + 1] if b + 1 < blocks else nothing
        out[b] = tile_product(tiles[b], tiles_own[b], before, after, parts[b])


def image_blocks(odd, edge_tiles, sides, linear, near_face, far_face, near_block, far_block):
    blocks, nodes, _ = linear.shape
    faces = near_face.shape[2]
    even = odd[1] == 0
    low = columns_split(jnp.where(even, far_block[...], near_block[...]))
    high = columns_split(jnp.where(even, near_block[...], far_block[...]))
    even = odd[0] == 0
    for b in range(blocks):
        new = linear[b]
        if b == 0:
            new = new + product(edge_tiles[0][:, :nodes], low)
        if b == blocks - 1:
            new = new + product(edge_tiles[1][:, nodes:], high)
        below = jnp.where(even, far_face[b], near_face[0, b])
        above = jnp.where(even, near_face[1, b], far_face[b])
        yield b, jnp.concatenate(
            [
                new[:faces] + sides[b, :faces] * below,
                new[faces : nodes - faces],
                new[nodes - faces :] + sides[b, faces:] * above,
            ],
            axis=0,
        )


def send_out(projected, spread, sems):
    return start_all([(projected, spread.at[i]) for i in range(spread.shape[0])], sems)


def image_kernel(odd, edge_tiles, sides, basis_rows, pair, residual, linear, far_face, near_face, near_block, far_block, image_out, rest_out, spread, start, near, far, image, rest, flat, projected, edges, sems, stores):
    blocks, nodes, _ = linear.shape
    for b, new in image_blocks(odd, edge_tiles, sides, linear, near_face, far_face, near_block, far_block):
        image[b] = new
        left = residual[b] - new
        rest[b] = left
        flat[b * nodes : (b + 1) * nodes] = columns_split(left)
    projected[...] = product(basis_rows[...], flat[...])
    copies = send_out(projected, spread, sems)
    for b in (0, blocks - 1, *range(1, blocks - 1)):
        start[b] = product(rows_split(pair[b][:, nodes:]), flat[b * nodes : (b + 1) * nodes])
        if b == blocks - 1:
            even = odd[1] == 0
            edges[0] = jnp.where(even, start[blocks - 1], start[0])
            edges[1] = jnp.where(even, start[0], start[blocks - 1])
            copies += start_all(
                [(edges.at[0], near), (edges.at[1], far), (image, image_out), (rest, rest_out)], stores
            )
    for copy in copies:
        copy.wait()


def first_kernel(odd, basis_in, coupling_in, pair_in, field_in, spread, near, far, basis, field, coupling, pair, residual, projected, sems, arrived, edges_arrived):
    blocks, nodes, columns = field.shape
    loads = start_all([(basis_in, basis), (field_in, field)], arrived)
    edge_loads = start_all(
        [
            (source.at[b], target.at[i])
            for source, target in ((pair_in, pair), (coupling_in, coupling), (field_in, residual))
            for i, b in enumerate((0, blocks - 1))
        ],
        edges_arrived,
    )
    for load in loads:
        load.wait()
    projected[...] = dot(basis[...], field[...].reshape(blocks * nodes, columns))
    copies = send_out(projected, spread, sems)
    for load in edge_loads:
        load.wait()
    even = odd[1] == 0
    start, beside, own = block_sweep(pair[0], coupling[0], residual[0])
    last, beyond, own_last = block_sweep(pair[1], coupling[1], residual[1])
    to_previous = jnp.concatenate([beside[:, :nodes], own], axis=1)
    to_next = jnp.concatenate([beyond[:, nodes:], own_last], axis=1)
    near[:nodes] = jnp.where(even, last, start)
    far[:nodes] = jnp.where(even, start, last)
    near[nodes:] = jnp.where(even, to_next, to_previous)
    far[nodes:] = jnp.where(even, to_previous, to_next)
    for copy in copies:
        copy.wait()


def sums_kernel(odd, edge_tiles, sides, image, rest, linear, far_face, near_face, near_block, far_block, sums):
    nodes, columns = linear.shape[1:]
    parts = [jnp.zeros((8, columns), jnp.float32) for _ in range(5)]

    def inner(left, right):
        return jnp.sum((left * right).reshape(nodes // 8, 8, columns), axis=0)

    for b, new in image_blocks(odd, edge_tiles, sides, linear, near_face, far_face, near_block, far_block):
        change = new * SCALE
        left, right = image[b], rest[b]
        for i, (x, y) in enumerate(((left, right), (left, left), (change, right), (change, left), (change, change))):
            parts[i] = parts[i] + inner(x, y)
    for i in range(5):
        sums[i : i + 1] = jnp.sum(parts[i], axis=0, keepdims=True)


def call(kernel, outs, scratch, *operands, slow=0):
    specs, given = [], []
    for at, operand in enumerate(operands):
        space = pltpu.HBM if at >= len(operands) - slow else pltpu.VMEM
        if operand.dtype == jnp.int32:
            space = pltpu.SMEM
        elif operand.size > 2 * operand.shape[-1] ** 2 or space is pltpu.HBM:
            operand = pltpu.with_memory_space_constraint(operand, space)
        specs.append(pl.BlockSpec(memory_space=space))
        given.append(operand)
    return pl.pallas_call(
        kernel,
        out_shape=[(space or jax.ShapeDtypeStruct)(shape, kind) for shape, kind, space in outs],
        in_specs=specs,
        out_specs=[pl.BlockSpec(memory_space=space or pltpu.VMEM) for _, _, space in outs],
        scratch_shapes=scratch,
        compiler_params=pltpu.CompilerParams(vmem_limit_bytes=12 << 20),
        cost_estimate=pl.CostEstimate(flops=1000, transcendentals=0, bytes_accessed=1000),
    )(*given)


def shards(forcing, coupling, diag_pair, side, basis, coarse_inverse):
    residual = forcing[0]
    basis_all = basis[0]
    blocks, nodes, columns = residual.shape
    faces = side.shape[2] // 2
    coarse, own_coarse = coarse_inverse.shape[2], coarse_inverse.shape[1]
    odd = jnp.stack([lax.axis_index("sec") % 2, lax.axis_index("sub") % 2]).astype(jnp.int32)
    wide, thin, fast = jnp.float32, jnp.bfloat16, pltpu.VMEM
    subs = lax.axis_size("sub")
    block = ((nodes, columns), wide, None)
    edge = ((nodes, columns), wide, pltpu.HBM)
    small = ((2 * nodes, columns), wide, None)
    field = ((blocks, nodes, columns), wide, fast)
    kept = ((blocks, nodes, columns), wide, pltpu.HBM)
    face = ((blocks, faces, columns), wide, fast)
    tile = ((blocks, 2 * nodes, 2 * nodes), thin)
    tile_own = ((blocks, nodes, 2 * nodes), thin)
    padded = pltpu.VMEM((blocks + 2, nodes, 2 * columns), thin)
    spread_out = ((subs, own_coarse, columns), wide, pltpu.HBM)
    spreading = [pltpu.VMEM((own_coarse, columns), wide), pltpu.SemaphoreType.DMA((subs,))]

    spread, near, far = call(
        first_kernel,
        [spread_out, small, small],
        [
            pltpu.VMEM(basis_all.shape, wide),
            pltpu.VMEM((blocks, nodes, columns), wide),
            *[pltpu.VMEM((2, nodes, columns), wide)] * 3,
            *spreading,
            pltpu.SemaphoreType.DMA((2,)),
            pltpu.SemaphoreType.DMA((6,)),
        ],
        odd, basis_all, coupling[0], diag_pair[0], residual,
        slow=4,
    )
    spread, odd, residual, coupling, diag_pair, side, basis_all = lax.optimization_barrier(
        (spread, odd, residual, coupling, diag_pair, side, basis_all)
    )
    pair = diag_pair[0]
    halo = swap(near, far, "sub")
    sweep, sweep_own, tiles, tiles_own, edge_tiles, start, sides, basis_rows, basis_columns, coarse_rows = call(
        prepare_kernel,
        [
            (*tile, fast),
            (*tile_own, fast),
            (*tile, pltpu.HBM),
            (*tile_own, pltpu.HBM),
            ((2, 2 * nodes, 2 * nodes), thin, pltpu.HBM),
            field,
            ((blocks, 2 * faces, columns), wide, pltpu.HBM),
            ((2 * own_coarse, blocks * nodes), thin, pltpu.HBM),
            ((blocks * nodes, 2 * own_coarse), thin, fast),
            ((2 * own_coarse, coarse), thin, fast),
        ],
        [
            pltpu.VMEM((blocks, nodes, columns), wide),
            pltpu.VMEM((blocks, nodes, columns), wide),
            pltpu.VMEM((blocks, nodes, columns), wide),
            pltpu.VMEM(basis_all.shape, wide),
            pltpu.VMEM((own_coarse, coarse), wide),
            pltpu.VMEM(*tile),
            pltpu.VMEM(*tile_own),
            pltpu.VMEM((blocks, 2 * faces, columns), wide),
            pltpu.VMEM((2 * own_coarse, blocks * nodes), thin),
            pltpu.SemaphoreType.DMA((5,)),
            pltpu.SemaphoreType.DMA((6,)),
        ],
        side[0], coupling[0], pair, residual, basis_all, coarse_inverse[0],
        slow=5,
    )

    def precondition(start, near, far, kept, spread):
        gathered = gather_sub(spread)
        (partial,) = call(first_sweep_kernel, [field], [], sweep, sweep_own, start)
        given = (odd, sweep, sweep_own, start, partial, far, near)
        if kept:
            (local,) = call(sweep_kernel, [field], [padded] * 2, *given, *kept)
        else:
            local, *kept = call(
                keeping_sweep_kernel,
                [field, edge, edge],
                [padded, padded, pltpu.SemaphoreType.DMA((2,))],
                *given,
            )
        update, near_face, far_face, near_block, far_block = call(
            update_kernel, [field, face, face, block, block], [], odd, coarse_rows, gathered, basis_columns, local
        )
        sections = lax.axis_size("sec")
        pairs = [[i, i + 1] for i in range(0, sections, 2)]
        faces_in = (
            lax.all_gather(near_face, "sec", axis_index_groups=pairs),
            lax.ppermute(far_face, "sec", pairings("sec")[1]),
        )
        blocks_in = swap(near_block, far_block, "sub")
        (linear,) = call(linear_kernel, [field], [], tiles, tiles_own, update)
        return kept, update, linear, faces_in[1], faces_in[0], *blocks_in

    kept_tiles, first, linear, *given = precondition(start, *halo, None, spread)
    image, rest, spread, start, near, far = call(
        image_kernel,
        [kept, kept, spread_out, field, edge, edge],
        [
            pltpu.VMEM((blocks, nodes, columns), wide),
            pltpu.VMEM((blocks, nodes, columns), wide),
            pltpu.VMEM((blocks * nodes, 2 * columns), thin),
            pltpu.VMEM((own_coarse, columns), wide),
            pltpu.VMEM((2, nodes, columns), wide),
            pltpu.SemaphoreType.DMA((subs,)),
            pltpu.SemaphoreType.DMA((4,)),
        ],
        odd, edge_tiles, sides, basis_rows, pair, residual, linear, *given,
    )
    _, second, linear, *given = precondition(start, *swap(near, far, "sub"), kept_tiles, spread)
    (sums,) = call(sums_kernel, [((5, columns), wide, fast)], [], odd, edge_tiles, sides, image, rest, linear, *given)
    sums = total(sums)
    short = -sums[0] / sums[1]
    step = 1.0 - short
    upper = step * (sums[2] + short * sums[3])
    scaled = step / SCALE
    lower = short * short * sums[1] + 2.0 * short * scaled * sums[3] + scaled * scaled * sums[4]
    step_next = upper / SCALE / lower
    result = (step + step_next * short) * first + (step_next * step) * second
    return result[None]


def solution(mesh):
    placed = (
        P("sec", "sub", None, None),
        P("sec", "sub", None, None),
        P("sec", "sub", None, None),
        P("sec", "sub", None),
        P("sec", "sub", None),
        P("sec", "sub", None),
    )
    return jax.shard_map(
        shards, mesh=mesh, in_specs=placed, out_specs=P("sec", "sub", None, None), check_vma=False
    )
```

```python
import jax
import jax.numpy as jnp
from jax import lax
from jax.experimental import pallas as pl
from jax.experimental.pallas import tpu as pltpu
from jax.sharding import PartitionSpec as P

SWEEPS = 4
SCALE = 2.0**-16

PRECISE = lax.Precision.HIGHEST


def dot(left, right):
    return jnp.dot(left, right, precision=PRECISE, preferred_element_type=jnp.float32)


def pairings(axis):
    count = lax.axis_size(axis)
    near = [(i, i ^ 1) for i in range(count)]
    low = [(i, i + 1) for i in range(1, count - 1, 2)]
    return near, low + [(target, source) for source, target in low]


def swap(to_near, to_far, axis):
    near, far = pairings(axis)
    from_far = lax.ppermute(to_far, axis, far)
    return lax.ppermute(to_near, axis, near), from_far


def gather_sub(spread):
    return lax.all_to_all(spread, "sub", 0, 0, tiled=True).reshape(-1, *spread.shape[2:])


def total(sums):
    sections, subs = lax.axis_size("sec"), lax.axis_size("sub")
    planes = sections // 4
    within = [
        [(4 * p + 2 * run + core) * subs + sub for run in range(2) for sub in range(subs)]
        for p in range(planes)
        for core in range(2)
    ]
    across = [[4 * p + 2 * run + core for p in range(planes) for core in range(2)] for run in range(2)]
    flat = sums.reshape(1, -1)
    for axes, groups in (("sec", across), (("sec", "sub"), within)):
        spread = jnp.broadcast_to(flat[None], (len(groups[0]), *flat.shape))
        flat = jnp.sum(lax.all_to_all(spread, axes, 0, 0, axis_index_groups=groups, tiled=True), axis=0)
    return flat.reshape(sums.shape)


def split(value):
    high = value.astype(jnp.bfloat16)
    return high, (value - high.astype(jnp.float32)).astype(jnp.bfloat16)


def rows_split(value):
    return jnp.concatenate(split(value), axis=0)


def columns_split(value):
    return jnp.concatenate(split(value), axis=1)


def product(rows, columns):
    all_four = jnp.dot(rows, columns, preferred_element_type=jnp.float32)
    half, width = all_four.shape[0] // 2, all_four.shape[1] // 2
    top = all_four[:half, :width] + (all_four[:half, width:] + all_four[half:, :width])
    return top + all_four[half:, width:]


def pair_split(value):
    high, low = split(value)
    both = jnp.concatenate([high.astype(jnp.float32), low.astype(jnp.float32)], axis=1)
    return both.astype(jnp.bfloat16)


def pair_product(pairs, columns):
    both = jnp.dot(pairs, jnp.concatenate([columns, columns], axis=0), preferred_element_type=jnp.float32)
    width = both.shape[1] // 2
    return both[:, :width] + both[:, width:]


def tile_product(beside, centre, before, after, own):
    return product(beside, jnp.concatenate([before, after], axis=0)) + pair_product(centre, own)


def block_sweep(pair, coupling, field):
    nodes = pair.shape[0]
    inverse = rows_split(pair[:, nodes:])
    row = lax.broadcasted_iota(jnp.int32, (nodes, nodes), 0)
    unit = (row == lax.broadcasted_iota(jnp.int32, (nodes, nodes), 1)).astype(jnp.float32)
    beside = -product(inverse, columns_split(coupling))
    own = unit - product(inverse, columns_split(pair))[:, :nodes]
    return product(inverse, columns_split(field)), beside, own


def start_all(pairs, sems):
    loads = [pltpu.make_async_copy(source, target, sems.at[i]) for i, (source, target) in enumerate(pairs)]
    for load in loads:
        load.start()
    return loads


def prepare_kernel(side, coupling_in, pair_in, residual_in, basis_in, inverse_in, sweep, sweep_own, tiles_out, tiles_own_out, edge_tiles_out, start, sides_out, basis_rows_out, basis_columns, coarse_rows, coupling, pair, residual, basis, inverse_rows, tiles, tiles_own, sides, basis_rows, sems, stores):
    blocks, nodes, columns = residual.shape
    loads = start_all(
        [
            (pair_in, pair),
            (coupling_in, coupling),
            (residual_in, residual),
            (inverse_in, inverse_rows),
            (basis_in, basis),
        ],
        sems,
    )
    for load in loads[:3]:
        load.wait()
    for b in range(blocks):
        start[b], beside, own = block_sweep(pair[b], coupling[b], residual[b])
        sweep[b] = rows_split(beside)
        sweep_own[b] = pair_split(own)
        tiles[b] = rows_split(coupling[b])
        tiles_own[b] = pair_split(pair[b][:, :nodes])
        sides[b] = jnp.broadcast_to(side[b : b + 1].T, sides.shape[1:])
    for load in loads[3:]:
        load.wait()
    parts = rows_split(basis[...])
    basis_rows[...] = parts
    copies = start_all(
        [
            (tiles, tiles_out),
            (tiles_own, tiles_own_out),
            (sides, sides_out),
            (basis_rows, basis_rows_out),
            (tiles.at[0], edge_tiles_out.at[0]),
            (tiles.at[blocks - 1], edge_tiles_out.at[1]),
        ],
        stores,
    )
    coarse_rows[...] = rows_split(inverse_rows[...])
    basis_columns[...] = parts.astype(jnp.float32).T.astype(jnp.bfloat16)
    for copy in copies:
        copy.wait()


def inner_sweeps_kernel(tiles, tiles_own, start, out, first_ends):
    blocks, nodes, _ = start.shape
    parts = [columns_split(start[b]) for b in range(blocks)]
    nothing = jnp.zeros_like(parts[0])
    for sweep in range(SWEEPS - 1):
        new = [
            start[b]
            + tile_product(
                tiles[b],
                tiles_own[b],
                parts[b - 1] if b else nothing,
                parts[b + 1] if b + 1 < blocks else nothing,
                parts[b],
            )
            for b in range(blocks)
        ]
        if sweep == 0:
            first_ends[0], first_ends[1] = new[0], new[-1]
        if sweep < SWEEPS - 2:
            parts = [columns_split(value) for value in new]
    for b in range(blocks):
        out[b] = new[b]


def outer_sweeps_kernel(odd, tiles, tiles_own, start, inner, first_ends, far, near, far_tile, near_tile, out):
    blocks, nodes, _ = start.shape
    even = odd[1] == 0
    far_tile, near_tile = far_tile[-nodes:], near_tile[-nodes:]
    ends = (
        (0, 1, jnp.where(even, far[:nodes], near[:nodes]), jnp.where(even, far_tile, near_tile)),
        (blocks - 1, -1, jnp.where(even, near[:nodes], far[:nodes]), jnp.where(even, near_tile, far_tile)),
    )
    for at, (end, inward, beside, tile) in enumerate(ends):
        tile = rows_split(tile)

        def of_block(b, outer, own=None, deeper=None):
            lower, upper = tiles[b][:, :nodes], tiles[b][:, nodes:]
            total = product(lower if inward == 1 else upper, outer)
            if own is not None:
                total = total + pair_product(tiles_own[b], own)
            if deeper is not None:
                total = total + product(upper if inward == 1 else lower, deeper)
            return total

        def of_beside(edge, last):
            return beside + product(tile, jnp.concatenate([columns_split(edge), last], axis=0))

        one, two, three = end, end + inward, end + 2 * inward
        beside_0 = columns_split(beside)
        first = of_block(one, beside_0)
        beside_1 = columns_split(of_beside(start[one], beside_0))
        beside_2 = columns_split(of_beside(first_ends[at] + first, beside_1))
        first = columns_split(first)
        second = columns_split(of_block(one, beside_1, first))
        second_two = columns_split(of_block(two, first))
        out[one] = inner[one] + of_block(one, beside_2, second, second_two)
        out[two] = inner[two] + of_block(two, second, second_two)
        out[three] = inner[three] + of_block(three, second_two)
    for b in range(3, blocks - 3):
        out[b] = inner[b]


def update_kernel(odd, coarse_rows, gathered, basis_columns, local, update, near_face, far_face, near_block, far_block):
    blocks, nodes, _ = local.shape
    faces = near_face.shape[1]
    correction = columns_split(product(coarse_rows[...], columns_split(gathered[...])))
    for b in range(blocks):
        new = local[b] + pair_product(basis_columns[b * nodes : (b + 1) * nodes], correction)
        update[b] = new
        south, north = new[:faces], new[nodes - faces :]
        even = odd[0] == 0
        near_face[b] = jnp.where(even, north, south)
        far_face[b] = jnp.where(even, south, north)
    even = odd[1] == 0
    near_block[...] = jnp.where(even, update[blocks - 1], update[0])
    far_block[...] = jnp.where(even, update[0], update[blocks - 1])


def keeping_update_kernel(odd, coarse_rows, gathered, basis_columns, local, far, near, update, near_face, far_face, near_block, far_block, far_kept, near_kept, sems):
    nodes = local.shape[1]
    copies = start_all([(far.at[nodes : 2 * nodes], far_kept), (near.at[nodes : 2 * nodes], near_kept)], sems)
    update_kernel(
        odd, coarse_rows, gathered, basis_columns, local, update, near_face, far_face, near_block, far_block
    )
    for copy in copies:
        copy.wait()


def linear_kernel(tiles, tiles_own, update, out):
    blocks = update.shape[0]
    parts = [columns_split(update[b]) for b in range(blocks)]
    nothing = jnp.zeros_like(parts[0])
    for b in range(blocks):
        before = parts[b - 1] if b else nothing
        after = parts[b + 1] if b + 1 < blocks else nothing
        out[b] = tile_product(tiles[b], tiles_own[b], before, after, parts[b])


def image_blocks(odd, edge_tiles, sides, linear, near_face, far_face, near_block, far_block):
    blocks, nodes, _ = linear.shape
    faces = near_face.shape[2]
    even = odd[1] == 0
    low = columns_split(jnp.where(even, far_block[...], near_block[...]))
    high = columns_split(jnp.where(even, near_block[...], far_block[...]))
    even = odd[0] == 0
    for b in range(blocks):
        new = linear[b]
        if b == 0:
            new = new + product(edge_tiles[0][:, :nodes], low)
        if b == blocks - 1:
            new = new + product(edge_tiles[1][:, nodes:], high)
        below = jnp.where(even, far_face[b], near_face[0, b])
        above = jnp.where(even, near_face[1, b], far_face[b])
        yield b, jnp.concatenate(
            [
                new[:faces] + sides[b, :faces] * below,
                new[faces : nodes - faces],
                new[nodes - faces :] + sides[b, faces:] * above,
            ],
            axis=0,
        )


def send_out(projected, spread, sems):
    return start_all([(projected, spread.at[i]) for i in range(spread.shape[0])], sems)


def image_kernel(odd, edge_tiles, sides, basis_rows, pair, residual, linear, far_face, near_face, near_block, far_block, image_out, rest_out, spread, start, near, far, image, rest, flat, projected, edges, sems, stores):
    blocks, nodes, _ = linear.shape
    for b, new in image_blocks(odd, edge_tiles, sides, linear, near_face, far_face, near_block, far_block):
        image[b] = new
        left = residual[b] - new
        rest[b] = left
        flat[b * nodes : (b + 1) * nodes] = columns_split(left)
    projected[...] = product(basis_rows[...], flat[...])
    copies = send_out(projected, spread, sems)
    for b in (0, blocks - 1, *range(1, blocks - 1)):
        start[b] = product(rows_split(pair[b][:, nodes:]), flat[b * nodes : (b + 1) * nodes])
        if b == blocks - 1:
            even = odd[1] == 0
            edges[0] = jnp.where(even, start[blocks - 1], start[0])
            edges[1] = jnp.where(even, start[0], start[blocks - 1])
            copies += start_all(
                [(edges.at[0], near), (edges.at[1], far), (image, image_out), (rest, rest_out)], stores
            )
    for copy in copies:
        copy.wait()


def first_kernel(odd, basis_in, coupling_in, pair_in, field_in, spread, near, far, basis, field, coupling, pair, residual, projected, sems, arrived, edges_arrived):
    blocks, nodes, columns = field.shape
    edge_loads = start_all(
        [
            (source.at[b], target.at[i])
            for source, target in ((pair_in, pair), (coupling_in, coupling), (field_in, residual))
            for i, b in enumerate((0, blocks - 1))
        ],
        edges_arrived,
    )
    loads = start_all([(basis_in, basis), (field_in, field)], arrived)
    for load in edge_loads:
        load.wait()
    even = odd[1] == 0
    start, beside, own = block_sweep(pair[0], coupling[0], residual[0])
    last, beyond, own_last = block_sweep(pair[1], coupling[1], residual[1])
    to_previous = jnp.concatenate([beside[:, :nodes], own], axis=1)
    to_next = jnp.concatenate([beyond[:, nodes:], own_last], axis=1)
    near[:nodes] = jnp.where(even, last, start)
    far[:nodes] = jnp.where(even, start, last)
    near[nodes:] = jnp.where(even, to_next, to_previous)
    far[nodes:] = jnp.where(even, to_previous, to_next)
    for load in loads:
        load.wait()
    projected[...] = dot(basis[...], field[...].reshape(blocks * nodes, columns))
    for copy in send_out(projected, spread, sems):
        copy.wait()


def sums_kernel(odd, edge_tiles, sides, image, rest, linear, far_face, near_face, near_block, far_block, sums):
    nodes, columns = linear.shape[1:]
    parts = [jnp.zeros((8, columns), jnp.float32) for _ in range(5)]

    def inner(left, right):
        return jnp.sum((left * right).reshape(nodes // 8, 8, columns), axis=0)

    for b, new in image_blocks(odd, edge_tiles, sides, linear, near_face, far_face, near_block, far_block):
        change = new * SCALE
        left, right = image[b], rest[b]
        for i, (x, y) in enumerate(((left, right), (left, left), (change, right), (change, left), (change, change))):
            parts[i] = parts[i] + inner(x, y)
    for i in range(5):
        sums[i : i + 1] = jnp.sum(parts[i], axis=0, keepdims=True)


def call(kernel, outs, scratch, *operands, slow=0):
    specs, given = [], []
    for at, operand in enumerate(operands):
        space = pltpu.HBM if at >= len(operands) - slow else pltpu.VMEM
        if operand.dtype == jnp.int32:
            space = pltpu.SMEM
        elif operand.size > 2 * operand.shape[-1] ** 2 or space is pltpu.HBM:
            operand = pltpu.with_memory_space_constraint(operand, space)
        specs.append(pl.BlockSpec(memory_space=space))
        given.append(operand)
    return pl.pallas_call(
        kernel,
        out_shape=[(space or jax.ShapeDtypeStruct)(shape, kind) for shape, kind, space in outs],
        in_specs=specs,
        out_specs=[pl.BlockSpec(memory_space=space or pltpu.VMEM) for _, _, space in outs],
        scratch_shapes=scratch,
        compiler_params=pltpu.CompilerParams(vmem_limit_bytes=12 << 20),
        cost_estimate=pl.CostEstimate(flops=1000, transcendentals=0, bytes_accessed=1000),
    )(*given)


def shards(forcing, coupling, diag_pair, side, basis, coarse_inverse):
    residual = forcing[0]
    basis_all = basis[0]
    blocks, nodes, columns = residual.shape
    faces = side.shape[2] // 2
    coarse, own_coarse = coarse_inverse.shape[2], coarse_inverse.shape[1]
    odd = jnp.stack([lax.axis_index("sec") % 2, lax.axis_index("sub") % 2]).astype(jnp.int32)
    wide, thin, fast = jnp.float32, jnp.bfloat16, pltpu.VMEM
    subs = lax.axis_size("sub")
    block = ((nodes, columns), wide, None)
    edge = ((nodes, columns), wide, pltpu.HBM)
    small = ((2 * nodes, columns), wide, None)
    field = ((blocks, nodes, columns), wide, fast)
    kept = ((blocks, nodes, columns), wide, pltpu.HBM)
    face = ((blocks, faces, columns), wide, fast)
    tile = ((blocks, 2 * nodes, 2 * nodes), thin)
    tile_own = ((blocks, nodes, 2 * nodes), thin)
    spread_out = ((subs, own_coarse, columns), wide, pltpu.HBM)
    spreading = [pltpu.VMEM((own_coarse, columns), wide), pltpu.SemaphoreType.DMA((subs,))]

    spread, near, far = call(
        first_kernel,
        [spread_out, small, small],
        [
            pltpu.VMEM(basis_all.shape, wide),
            pltpu.VMEM((blocks, nodes, columns), wide),
            *[pltpu.VMEM((2, nodes, columns), wide)] * 3,
            *spreading,
            pltpu.SemaphoreType.DMA((2,)),
            pltpu.SemaphoreType.DMA((6,)),
        ],
        odd, basis_all, coupling[0], diag_pair[0], residual,
        slow=4,
    )
    spread, odd, residual, coupling, diag_pair, side, basis_all = lax.optimization_barrier(
        (spread, odd, residual, coupling, diag_pair, side, basis_all)
    )
    pair = diag_pair[0]
    halo = swap(near, far, "sub")
    sweep, sweep_own, tiles, tiles_own, edge_tiles, start, sides, basis_rows, basis_columns, coarse_rows = call(
        prepare_kernel,
        [
            (*tile, fast),
            (*tile_own, fast),
            (*tile, pltpu.HBM),
            (*tile_own, pltpu.HBM),
            ((2, 2 * nodes, 2 * nodes), thin, pltpu.HBM),
            field,
            ((blocks, 2 * faces, columns), wide, pltpu.HBM),
            ((2 * own_coarse, blocks * nodes), thin, pltpu.HBM),
            ((blocks * nodes, 2 * own_coarse), thin, fast),
            ((2 * own_coarse, coarse), thin, fast),
        ],
        [
            pltpu.VMEM((blocks, nodes, columns), wide),
            pltpu.VMEM((blocks, nodes, columns), wide),
            pltpu.VMEM((blocks, nodes, columns), wide),
            pltpu.VMEM(basis_all.shape, wide),
            pltpu.VMEM((own_coarse, coarse), wide),
            pltpu.VMEM(*tile),
            pltpu.VMEM(*tile_own),
            pltpu.VMEM((blocks, 2 * faces, columns), wide),
            pltpu.VMEM((2 * own_coarse, blocks * nodes), thin),
            pltpu.SemaphoreType.DMA((5,)),
            pltpu.SemaphoreType.DMA((6,)),
        ],
        side[0], coupling[0], pair, residual, basis_all, coarse_inverse[0],
        slow=5,
    )

    def precondition(start, near, far, kept, spread):
        gathered = gather_sub(spread)
        inner, first_ends = call(
            inner_sweeps_kernel, [field, ((2, nodes, columns), wide, None)], [], sweep, sweep_own, start
        )
        (local,) = call(
            outer_sweeps_kernel, [field], [], odd, sweep, sweep_own, start, inner, first_ends, far, near, *(kept or (far, near))
        )
        outs = [field, face, face, block, block]
        given = (odd, coarse_rows, gathered, basis_columns, local)
        if kept:
            update, near_face, far_face, near_block, far_block = call(update_kernel, outs, [], *given)
        else:
            update, near_face, far_face, near_block, far_block, *kept = call(
                keeping_update_kernel, [*outs, edge, edge], [pltpu.SemaphoreType.DMA((2,))], *given, far, near
            )
        sections = lax.axis_size("sec")
        pairs = [[i, i + 1] for i in range(0, sections, 2)]
        faces_in = (
            lax.all_gather(near_face, "sec", axis_index_groups=pairs),
            lax.ppermute(far_face, "sec", pairings("sec")[1]),
        )
        blocks_in = swap(near_block, far_block, "sub")
        (linear,) = call(linear_kernel, [field], [], tiles, tiles_own, update)
        return kept, update, linear, faces_in[1], faces_in[0], *blocks_in

    kept_tiles, first, linear, *given = precondition(start, *halo, None, spread)
    image, rest, spread, start, near, far = call(
        image_kernel,
        [kept, kept, spread_out, field, edge, edge],
        [
            pltpu.VMEM((blocks, nodes, columns), wide),
            pltpu.VMEM((blocks, nodes, columns), wide),
            pltpu.VMEM((blocks * nodes, 2 * columns), thin),
            pltpu.VMEM((own_coarse, columns), wide),
            pltpu.VMEM((2, nodes, columns), wide),
            pltpu.SemaphoreType.DMA((subs,)),
            pltpu.SemaphoreType.DMA((4,)),
        ],
        odd, edge_tiles, sides, basis_rows, pair, residual, linear, *given,
    )
    _, second, linear, *given = precondition(start, *swap(near, far, "sub"), kept_tiles, spread)
    (sums,) = call(sums_kernel, [((5, columns), wide, fast)], [], odd, edge_tiles, sides, image, rest, linear, *given)
    sums = total(sums)
    short = -sums[0] / sums[1]
    step = 1.0 - short
    upper = step * (sums[2] + short * sums[3])
    scaled = step / SCALE
    lower = short * short * sums[1] + 2.0 * short * scaled * sums[3] + scaled * scaled * sums[4]
    step_next = upper / SCALE / lower
    result = (step + step_next * short) * first + (step_next * step) * second
    return result[None]


def solution(mesh):
    placed = (
        P("sec", "sub", None, None),
        P("sec", "sub", None, None),
        P("sec", "sub", None, None),
        P("sec", "sub", None),
        P("sec", "sub", None),
        P("sec", "sub", None),
    )
    return jax.shard_map(
        shards, mesh=mesh, in_specs=placed, out_specs=P("sec", "sub", None, None), check_vma=False
    )
```

```python
import jax
import jax.numpy as jnp
from jax import lax
from jax.experimental import pallas as pl
from jax.experimental.pallas import tpu as pltpu
from jax.sharding import PartitionSpec as P

SWEEPS = 4
SCALE = 2.0**-16

PRECISE = lax.Precision.HIGHEST


def dot(left, right):
    return jnp.dot(left, right, precision=PRECISE, preferred_element_type=jnp.float32)


def pairings(axis):
    count = lax.axis_size(axis)
    near = [(i, i ^ 1) for i in range(count)]
    low = [(i, i + 1) for i in range(1, count - 1, 2)]
    return near, low + [(target, source) for source, target in low]


def swap(to_near, to_far, axis):
    near, far = pairings(axis)
    from_far = lax.ppermute(to_far, axis, far)
    return lax.ppermute(to_near, axis, near), from_far


def gather_sub(spread):
    return lax.all_to_all(spread, "sub", 0, 0, tiled=True).reshape(-1, *spread.shape[2:])


def total(sums):
    sections, subs = lax.axis_size("sec"), lax.axis_size("sub")
    planes = sections // 4
    within = [
        [(4 * p + 2 * run + core) * subs + sub for run in range(2) for sub in range(subs)]
        for p in range(planes)
        for core in range(2)
    ]
    across = [[4 * p + 2 * run + core for p in range(planes) for core in range(2)] for run in range(2)]
    flat = sums.reshape(1, -1)
    for axes, groups in (("sec", across), (("sec", "sub"), within)):
        spread = jnp.broadcast_to(flat[None], (len(groups[0]), *flat.shape))
        flat = jnp.sum(lax.all_to_all(spread, axes, 0, 0, axis_index_groups=groups, tiled=True), axis=0)
    return flat.reshape(sums.shape)


def split(value):
    high = value.astype(jnp.bfloat16)
    return high, (value - high.astype(jnp.float32)).astype(jnp.bfloat16)


def rows_split(value):
    return jnp.concatenate(split(value), axis=0)


def columns_split(value):
    return jnp.concatenate(split(value), axis=1)


def product(rows, columns):
    all_four = jnp.dot(rows, columns, preferred_element_type=jnp.float32)
    half, width = all_four.shape[0] // 2, all_four.shape[1] // 2
    top = all_four[:half, :width] + (all_four[:half, width:] + all_four[half:, :width])
    return top + all_four[half:, width:]


def pair_split(value):
    high, low = split(value)
    both = jnp.concatenate([high.astype(jnp.float32), low.astype(jnp.float32)], axis=1)
    return both.astype(jnp.bfloat16)


def pair_product(pairs, columns):
    both = jnp.dot(pairs, jnp.concatenate([columns, columns], axis=0), preferred_element_type=jnp.float32)
    width = both.shape[1] // 2
    return both[:, :width] + both[:, width:]


def tile_product(beside, centre, before, after, own):
    return product(beside, jnp.concatenate([before, after], axis=0)) + pair_product(centre, own)


def block_sweep(pair, coupling, field):
    nodes = pair.shape[0]
    inverse = rows_split(pair[:, nodes:])
    row = lax.broadcasted_iota(jnp.int32, (nodes, nodes), 0)
    unit = (row == lax.broadcasted_iota(jnp.int32, (nodes, nodes), 1)).astype(jnp.float32)
    beside = -product(inverse, columns_split(coupling))
    own = unit - product(inverse, columns_split(pair))[:, :nodes]
    return product(inverse, columns_split(field)), beside, own


def start_all(pairs, sems):
    loads = [pltpu.make_async_copy(source, target, sems.at[i]) for i, (source, target) in enumerate(pairs)]
    for load in loads:
        load.start()
    return loads


def edge_kernel(odd, coupling_in, pair_in, residual_in, near, far, coupling, pair, residual, sems):
    blocks, nodes = pair_in.shape[:2]
    loads = start_all(
        [
            (source.at[b], target.at[i])
            for source, target in ((pair_in, pair), (coupling_in, coupling), (residual_in, residual))
            for i, b in enumerate((0, blocks - 1))
        ],
        sems,
    )
    for load in loads:
        load.wait()
    even = odd[1] == 0
    start, beside, own = block_sweep(pair[0], coupling[0], residual[0])
    last, beyond, own_last = block_sweep(pair[1], coupling[1], residual[1])
    to_previous = jnp.concatenate([beside[:, :nodes], own], axis=1)
    to_next = jnp.concatenate([beyond[:, nodes:], own_last], axis=1)
    near[:nodes] = jnp.where(even, last, start)
    far[:nodes] = jnp.where(even, start, last)
    near[nodes:] = jnp.where(even, to_next, to_previous)
    far[nodes:] = jnp.where(even, to_previous, to_next)


def prepare_kernel(side, coupling_in, pair_in, residual_in, basis_in, inverse_in, sweep, sweep_own, tiles_out, tiles_own_out, edge_tiles_out, start, sides_out, basis_rows_out, basis_columns, coarse_rows, coupling, pair, residual, basis, inverse_rows, tiles, tiles_own, sides, basis_rows, sems, stores):
    blocks, nodes, columns = residual.shape
    loads = start_all(
        [
            (pair_in, pair),
            (coupling_in, coupling),
            (residual_in, residual),
            (inverse_in, inverse_rows),
            (basis_in, basis),
        ],
        sems,
    )
    for load in loads[:3]:
        load.wait()
    for b in range(blocks):
        start[b], beside, own = block_sweep(pair[b], coupling[b], residual[b])
        sweep[b] = rows_split(beside)
        sweep_own[b] = pair_split(own)
        tiles[b] = rows_split(coupling[b])
        tiles_own[b] = pair_split(pair[b][:, :nodes])
        sides[b] = jnp.broadcast_to(side[b : b + 1].T, sides.shape[1:])
    for load in loads[3:]:
        load.wait()
    parts = rows_split(basis[...])
    basis_rows[...] = parts
    copies = start_all(
        [
            (tiles, tiles_out),
            (tiles_own, tiles_own_out),
            (sides, sides_out),
            (basis_rows, basis_rows_out),
            (tiles.at[0], edge_tiles_out.at[0]),
            (tiles.at[blocks - 1], edge_tiles_out.at[1]),
        ],
        stores,
    )
    coarse_rows[...] = rows_split(inverse_rows[...])
    basis_columns[...] = parts.astype(jnp.float32).T.astype(jnp.bfloat16)
    for copy in copies:
        copy.wait()


def inner_sweeps_kernel(tiles, tiles_own, start, out, first_ends):
    blocks, nodes, _ = start.shape
    parts = [columns_split(start[b]) for b in range(blocks)]
    nothing = jnp.zeros_like(parts[0])
    for sweep in range(SWEEPS - 1):
        new = [
            start[b]
            + tile_product(
                tiles[b],
                tiles_own[b],
                parts[b - 1] if b else nothing,
                parts[b + 1] if b + 1 < blocks else nothing,
                parts[b],
            )
            for b in range(blocks)
        ]
        if sweep == 0:
            first_ends[0], first_ends[1] = new[0], new[-1]
        if sweep < SWEEPS - 2:
            parts = [columns_split(value) for value in new]
    for b in range(blocks):
        out[b] = new[b]


def outer_sweeps_kernel(odd, tiles, tiles_own, start, inner, first_ends, far, near, far_tile, near_tile, out):
    blocks, nodes, _ = start.shape
    even = odd[1] == 0
    far_tile, near_tile = far_tile[-nodes:], near_tile[-nodes:]
    ends = (
        (0, 1, jnp.where(even, far[:nodes], near[:nodes]), jnp.where(even, far_tile, near_tile)),
        (blocks - 1, -1, jnp.where(even, near[:nodes], far[:nodes]), jnp.where(even, near_tile, far_tile)),
    )
    for at, (end, inward, beside, tile) in enumerate(ends):
        tile = rows_split(tile)

        def of_block(b, outer, own=None, deeper=None):
            lower, upper = tiles[b][:, :nodes], tiles[b][:, nodes:]
            total = product(lower if inward == 1 else upper, outer)
            if own is not None:
                total = total + pair_product(tiles_own[b], own)
            if deeper is not None:
                total = total + product(upper if inward == 1 else lower, deeper)
            return total

        def of_beside(edge, last):
            return beside + product(tile, jnp.concatenate([columns_split(edge), last], axis=0))

        one, two, three = end, end + inward, end + 2 * inward
        beside_0 = columns_split(beside)
        first = of_block(one, beside_0)
        beside_1 = columns_split(of_beside(start[one], beside_0))
        beside_2 = columns_split(of_beside(first_ends[at] + first, beside_1))
        first = columns_split(first)
        second = columns_split(of_block(one, beside_1, first))
        second_two = columns_split(of_block(two, first))
        out[one] = inner[one] + of_block(one, beside_2, second, second_two)
        out[two] = inner[two] + of_block(two, second, second_two)
        out[three] = inner[three] + of_block(three, second_two)
    for b in range(3, blocks - 3):
        out[b] = inner[b]


def update_kernel(odd, coarse_rows, gathered, basis_columns, local, update, near_face, far_face, near_block, far_block):
    blocks, nodes, _ = local.shape
    faces = near_face.shape[1]
    correction = columns_split(product(coarse_rows[...], columns_split(gathered[...])))
    for b in range(blocks):
        new = local[b] + pair_product(basis_columns[b * nodes : (b + 1) * nodes], correction)
        update[b] = new
        south, north = new[:faces], new[nodes - faces :]
        even = odd[0] == 0
        near_face[b] = jnp.where(even, north, south)
        far_face[b] = jnp.where(even, south, north)
    even = odd[1] == 0
    near_block[...] = jnp.where(even, update[blocks - 1], update[0])
    far_block[...] = jnp.where(even, update[0], update[blocks - 1])


def keeping_update_kernel(odd, coarse_rows, gathered, basis_columns, local, far, near, update, near_face, far_face, near_block, far_block, far_kept, near_kept, sems):
    nodes = local.shape[1]
    copies = start_all([(far.at[nodes : 2 * nodes], far_kept), (near.at[nodes : 2 * nodes], near_kept)], sems)
    update_kernel(
        odd, coarse_rows, gathered, basis_columns, local, update, near_face, far_face, near_block, far_block
    )
    for copy in copies:
        copy.wait()


def linear_kernel(tiles, tiles_own, update, out):
    blocks = update.shape[0]
    parts = [columns_split(update[b]) for b in range(blocks)]
    nothing = jnp.zeros_like(parts[0])
    for b in range(blocks):
        before = parts[b - 1] if b else nothing
        after = parts[b + 1] if b + 1 < blocks else nothing
        out[b] = tile_product(tiles[b], tiles_own[b], before, after, parts[b])


def image_blocks(odd, edge_tiles, sides, linear, near_face, far_face, near_block, far_block):
    blocks, nodes, _ = linear.shape
    faces = near_face.shape[2]
    even = odd[1] == 0
    low = columns_split(jnp.where(even, far_block[...], near_block[...]))
    high = columns_split(jnp.where(even, near_block[...], far_block[...]))
    even = odd[0] == 0
    for b in range(blocks):
        new = linear[b]
        if b == 0:
            new = new + product(edge_tiles[0][:, :nodes], low)
        if b == blocks - 1:
            new = new + product(edge_tiles[1][:, nodes:], high)
        below = jnp.where(even, far_face[b], near_face[0, b])
        above = jnp.where(even, near_face[1, b], far_face[b])
        yield b, jnp.concatenate(
            [
                new[:faces] + sides[b, :faces] * below,
                new[faces : nodes - faces],
                new[nodes - faces :] + sides[b, faces:] * above,
            ],
            axis=0,
        )


def send_out(projected, spread, sems):
    return start_all([(projected, spread.at[i]) for i in range(spread.shape[0])], sems)


def image_kernel(odd, edge_tiles, sides, basis_rows, pair, residual, linear, far_face, near_face, near_block, far_block, image_out, rest_out, spread, start, near, far, image, rest, flat, projected, edges, sems, stores):
    blocks, nodes, _ = linear.shape
    for b, new in image_blocks(odd, edge_tiles, sides, linear, near_face, far_face, near_block, far_block):
        image[b] = new
        left = residual[b] - new
        rest[b] = left
        flat[b * nodes : (b + 1) * nodes] = columns_split(left)
    projected[...] = product(basis_rows[...], flat[...])
    copies = send_out(projected, spread, sems)
    for b in (0, blocks - 1, *range(1, blocks - 1)):
        start[b] = product(rows_split(pair[b][:, nodes:]), flat[b * nodes : (b + 1) * nodes])
        if b == blocks - 1:
            even = odd[1] == 0
            edges[0] = jnp.where(even, start[blocks - 1], start[0])
            edges[1] = jnp.where(even, start[0], start[blocks - 1])
            copies += start_all(
                [(edges.at[0], near), (edges.at[1], far), (image, image_out), (rest, rest_out)], stores
            )
    for copy in copies:
        copy.wait()


def project_kernel(basis_in, field_in, spread, basis, field, projected, sems, arrived):
    blocks, nodes, columns = field.shape
    for load in start_all([(basis_in, basis), (field_in, field)], arrived):
        load.wait()
    projected[...] = dot(basis[...], field[...].reshape(blocks * nodes, columns))
    for copy in send_out(projected, spread, sems):
        copy.wait()


def sums_kernel(odd, edge_tiles, sides, image, rest, linear, far_face, near_face, near_block, far_block, sums):
    nodes, columns = linear.shape[1:]
    parts = [jnp.zeros((8, columns), jnp.float32) for _ in range(5)]

    def inner(left, right):
        return jnp.sum((left * right).reshape(nodes // 8, 8, columns), axis=0)

    for b, new in image_blocks(odd, edge_tiles, sides, linear, near_face, far_face, near_block, far_block):
        change = new * SCALE
        left, right = image[b], rest[b]
        for i, (x, y) in enumerate(((left, right), (left, left), (change, right), (change, left), (change, change))):
            parts[i] = parts[i] + inner(x, y)
    for i in range(5):
        sums[i : i + 1] = jnp.sum(parts[i], axis=0, keepdims=True)


def call(kernel, outs, scratch, *operands, slow=0):
    specs, given = [], []
    for at, operand in enumerate(operands):
        space = pltpu.HBM if at >= len(operands) - slow else pltpu.VMEM
        if operand.dtype == jnp.int32:
            space = pltpu.SMEM
        elif operand.size > 2 * operand.shape[-1] ** 2 or space is pltpu.HBM:
            operand = pltpu.with_memory_space_constraint(operand, space)
        specs.append(pl.BlockSpec(memory_space=space))
        given.append(operand)
    return pl.pallas_call(
        kernel,
        out_shape=[(space or jax.ShapeDtypeStruct)(shape, kind) for shape, kind, space in outs],
        in_specs=specs,
        out_specs=[pl.BlockSpec(memory_space=space or pltpu.VMEM) for _, _, space in outs],
        scratch_shapes=scratch,
        compiler_params=pltpu.CompilerParams(vmem_limit_bytes=12 << 20),
        cost_estimate=pl.CostEstimate(flops=1000, transcendentals=0, bytes_accessed=1000),
    )(*given)


def shards(forcing, coupling, diag_pair, side, basis, coarse_inverse):
    residual = forcing[0]
    basis_all = basis[0]
    blocks, nodes, columns = residual.shape
    faces = side.shape[2] // 2
    coarse, own_coarse = coarse_inverse.shape[2], coarse_inverse.shape[1]
    odd = jnp.stack([lax.axis_index("sec") % 2, lax.axis_index("sub") % 2]).astype(jnp.int32)
    wide, thin, fast = jnp.float32, jnp.bfloat16, pltpu.VMEM
    subs = lax.axis_size("sub")
    block = ((nodes, columns), wide, None)
    edge = ((nodes, columns), wide, pltpu.HBM)
    small = ((2 * nodes, columns), wide, None)
    field = ((blocks, nodes, columns), wide, fast)
    kept = ((blocks, nodes, columns), wide, pltpu.HBM)
    face = ((blocks, faces, columns), wide, fast)
    tile = ((blocks, 2 * nodes, 2 * nodes), thin)
    tile_own = ((blocks, nodes, 2 * nodes), thin)
    spread_out = ((subs, own_coarse, columns), wide, pltpu.HBM)
    spreading = [pltpu.VMEM((own_coarse, columns), wide), pltpu.SemaphoreType.DMA((subs,))]

    (spread,) = call(
        project_kernel,
        [spread_out],
        [
            pltpu.VMEM(basis_all.shape, wide),
            pltpu.VMEM((blocks, nodes, columns), wide),
            *spreading,
            pltpu.SemaphoreType.DMA((2,)),
        ],
        basis_all, residual,
        slow=2,
    )
    spread, odd, residual, coupling, diag_pair, side, basis_all = lax.optimization_barrier(
        (spread, odd, residual, coupling, diag_pair, side, basis_all)
    )
    pair = diag_pair[0]
    near, far = call(
        edge_kernel,
        [small, small],
        [pltpu.VMEM((2, nodes, columns), wide)] * 3 + [pltpu.SemaphoreType.DMA((6,))],
        odd, coupling[0], pair, residual,
        slow=3,
    )
    halo = swap(near, far, "sub")
    sweep, sweep_own, tiles, tiles_own, edge_tiles, start, sides, basis_rows, basis_columns, coarse_rows = call(
        prepare_kernel,
        [
            (*tile, fast),
            (*tile_own, fast),
            (*tile, pltpu.HBM),
            (*tile_own, pltpu.HBM),
            ((2, 2 * nodes, 2 * nodes), thin, pltpu.HBM),
            field,
            ((blocks, 2 * faces, columns), wide, pltpu.HBM),
            ((2 * own_coarse, blocks * nodes), thin, pltpu.HBM),
            ((blocks * nodes, 2 * own_coarse), thin, fast),
            ((2 * own_coarse, coarse), thin, fast),
        ],
        [
            pltpu.VMEM((blocks, nodes, columns), wide),
            pltpu.VMEM((blocks, nodes, columns), wide),
            pltpu.VMEM((blocks, nodes, columns), wide),
            pltpu.VMEM(basis_all.shape, wide),
            pltpu.VMEM((own_coarse, coarse), wide),
            pltpu.VMEM(*tile),
            pltpu.VMEM(*tile_own),
            pltpu.VMEM((blocks, 2 * faces, columns), wide),
            pltpu.VMEM((2 * own_coarse, blocks * nodes), thin),
            pltpu.SemaphoreType.DMA((5,)),
            pltpu.SemaphoreType.DMA((6,)),
        ],
        side[0], coupling[0], pair, residual, basis_all, coarse_inverse[0],
        slow=5,
    )

    def precondition(start, near, far, kept, spread):
        gathered = gather_sub(spread)
        inner, first_ends = call(
            inner_sweeps_kernel, [field, ((2, nodes, columns), wide, None)], [], sweep, sweep_own, start
        )
        (local,) = call(
            outer_sweeps_kernel, [field], [], odd, sweep, sweep_own, start, inner, first_ends, far, near, *(kept or (far, near))
        )
        outs = [field, face, face, block, block]
        given = (odd, coarse_rows, gathered, basis_columns, local)
        if kept:
            update, near_face, far_face, near_block, far_block = call(update_kernel, outs, [], *given)
        else:
            update, near_face, far_face, near_block, far_block, *kept = call(
                keeping_update_kernel, [*outs, edge, edge], [pltpu.SemaphoreType.DMA((2,))], *given, far, near
            )
        sections = lax.axis_size("sec")
        pairs = [[i, i + 1] for i in range(0, sections, 2)]
        faces_in = (
            lax.all_gather(near_face, "sec", axis_index_groups=pairs),
            lax.ppermute(far_face, "sec", pairings("sec")[1]),
        )
        blocks_in = swap(near_block, far_block, "sub")
        (linear,) = call(linear_kernel, [field], [], tiles, tiles_own, update)
        return kept, update, linear, faces_in[1], faces_in[0], *blocks_in

    kept_tiles, first, linear, *given = precondition(start, *halo, None, spread)
    image, rest, spread, start, near, far = call(
        image_kernel,
        [kept, kept, spread_out, field, edge, edge],
        [
            pltpu.VMEM((blocks, nodes, columns), wide),
            pltpu.VMEM((blocks, nodes, columns), wide),
            pltpu.VMEM((blocks * nodes, 2 * columns), thin),
            pltpu.VMEM((own_coarse, columns), wide),
            pltpu.VMEM((2, nodes, columns), wide),
            pltpu.SemaphoreType.DMA((subs,)),
            pltpu.SemaphoreType.DMA((4,)),
        ],
        odd, edge_tiles, sides, basis_rows, pair, residual, linear, *given,
    )
    _, second, linear, *given = precondition(start, *swap(near, far, "sub"), kept_tiles, spread)
    (sums,) = call(sums_kernel, [((5, columns), wide, fast)], [], odd, edge_tiles, sides, image, rest, linear, *given)
    sums = total(sums)
    short = -sums[0] / sums[1]
    step = 1.0 - short
    upper = step * (sums[2] + short * sums[3])
    scaled = step / SCALE
    lower = short * short * sums[1] + 2.0 * short * scaled * sums[3] + scaled * scaled * sums[4]
    step_next = upper / SCALE / lower
    result = (step + step_next * short) * first + (step_next * step) * second
    return result[None]


def solution(mesh):
    placed = (
        P("sec", "sub", None, None),
        P("sec", "sub", None, None),
        P("sec", "sub", None, None),
        P("sec", "sub", None),
        P("sec", "sub", None),
        P("sec", "sub", None),
    )
    return jax.shard_map(
        shards, mesh=mesh, in_specs=placed, out_specs=P("sec", "sub", None, None), check_vma=False
    )
```

```python
import jax
import jax.numpy as jnp
from jax import lax
from jax.experimental import pallas as pl
from jax.experimental.pallas import tpu as pltpu
from jax.sharding import PartitionSpec as P

SWEEPS = 4
SCALE = 2.0**-16

PRECISE = lax.Precision.HIGHEST


def dot(left, right):
    return jnp.dot(left, right, precision=PRECISE, preferred_element_type=jnp.float32)


def pairings(axis):
    count = lax.axis_size(axis)
    near = [(i, i ^ 1) for i in range(count)]
    low = [(i, i + 1) for i in range(1, count - 1, 2)]
    return near, low + [(target, source) for source, target in low]


def swap(to_near, to_far, axis):
    near, far = pairings(axis)
    from_far = lax.ppermute(to_far, axis, far)
    return lax.ppermute(to_near, axis, near), from_far


def gather_sub(spread):
    return lax.all_to_all(spread, "sub", 0, 0, tiled=True).reshape(-1, *spread.shape[2:])


def total(sums):
    sections, subs = lax.axis_size("sec"), lax.axis_size("sub")
    planes = sections // 4
    within = [
        [(4 * p + 2 * run + core) * subs + sub for run in range(2) for sub in range(subs)]
        for p in range(planes)
        for core in range(2)
    ]
    across = [[4 * p + 2 * run + core for p in range(planes) for core in range(2)] for run in range(2)]
    flat = sums.reshape(1, -1)
    for axes, groups in (("sec", across), (("sec", "sub"), within)):
        spread = jnp.broadcast_to(flat[None], (len(groups[0]), *flat.shape))
        flat = jnp.sum(lax.all_to_all(spread, axes, 0, 0, axis_index_groups=groups, tiled=True), axis=0)
    return flat.reshape(sums.shape)


def split(value):
    high = value.astype(jnp.bfloat16)
    return high, (value - high.astype(jnp.float32)).astype(jnp.bfloat16)


def rows_split(value):
    return jnp.concatenate(split(value), axis=0)


def columns_split(value):
    return jnp.concatenate(split(value), axis=1)


def product(rows, columns):
    all_four = jnp.dot(rows, columns, preferred_element_type=jnp.float32)
    half, width = all_four.shape[0] // 2, all_four.shape[1] // 2
    top = all_four[:half, :width] + (all_four[:half, width:] + all_four[half:, :width])
    return top + all_four[half:, width:]


def pair_split(value):
    high, low = split(value)
    both = jnp.concatenate([high.astype(jnp.float32), low.astype(jnp.float32)], axis=1)
    return both.astype(jnp.bfloat16)


def pair_product(pairs, columns):
    both = jnp.dot(pairs, jnp.concatenate([columns, columns], axis=0), preferred_element_type=jnp.float32)
    width = both.shape[1] // 2
    return both[:, :width] + both[:, width:]


def tile_product(beside, centre, before, after, own):
    return product(beside, jnp.concatenate([before, after], axis=0)) + pair_product(centre, own)


def block_sweep(pair, coupling, field):
    nodes = pair.shape[0]
    inverse = rows_split(pair[:, nodes:])
    row = lax.broadcasted_iota(jnp.int32, (nodes, nodes), 0)
    unit = (row == lax.broadcasted_iota(jnp.int32, (nodes, nodes), 1)).astype(jnp.float32)
    beside = -product(inverse, columns_split(coupling))
    own = unit - product(inverse, columns_split(pair))[:, :nodes]
    return product(inverse, columns_split(field)), beside, own


def start_all(pairs, sems):
    loads = [pltpu.make_async_copy(source, target, sems.at[i]) for i, (source, target) in enumerate(pairs)]
    for load in loads:
        load.start()
    return loads


def edge_kernel(odd, coupling_in, pair_in, residual_in, near, far, coupling, pair, residual, sems):
    blocks, nodes = pair_in.shape[:2]
    loads = start_all(
        [
            (source.at[b], target.at[i])
            for source, target in ((pair_in, pair), (coupling_in, coupling), (residual_in, residual))
            for i, b in enumerate((0, blocks - 1))
        ],
        sems,
    )
    for load in loads:
        load.wait()
    even = odd[1] == 0
    start, beside, own = block_sweep(pair[0], coupling[0], residual[0])
    last, beyond, own_last = block_sweep(pair[1], coupling[1], residual[1])
    to_previous = jnp.concatenate([beside[:, :nodes], own], axis=1)
    to_next = jnp.concatenate([beyond[:, nodes:], own_last], axis=1)
    near[:nodes] = jnp.where(even, last, start)
    far[:nodes] = jnp.where(even, start, last)
    near[nodes:] = jnp.where(even, to_next, to_previous)
    far[nodes:] = jnp.where(even, to_previous, to_next)


def prepare_kernel(side, coupling_in, pair_in, residual_in, basis_in, inverse_in, sweep, sweep_own, tiles_out, tiles_own_out, edge_tiles_out, start, sides_out, basis_rows_out, basis_columns, coarse_rows, coupling, pair, residual, basis, inverse_rows, tiles, tiles_own, sides, basis_rows, sems, stores):
    blocks, nodes, columns = residual.shape
    loads = start_all(
        [
            (pair_in, pair),
            (coupling_in, coupling),
            (residual_in, residual),
            (inverse_in, inverse_rows),
            (basis_in, basis),
        ],
        sems,
    )
    for load in loads[:3]:
        load.wait()
    for b in range(blocks):
        start[b], beside, own = block_sweep(pair[b], coupling[b], residual[b])
        sweep[b] = rows_split(beside)
        sweep_own[b] = pair_split(own)
        tiles[b] = rows_split(coupling[b])
        tiles_own[b] = pair_split(pair[b][:, :nodes])
        sides[b] = jnp.broadcast_to(side[b : b + 1].T, sides.shape[1:])
    for load in loads[3:]:
        load.wait()
    parts = rows_split(basis[...])
    basis_rows[...] = parts
    copies = start_all(
        [
            (tiles, tiles_out),
            (tiles_own, tiles_own_out),
            (sides, sides_out),
            (basis_rows, basis_rows_out),
            (tiles.at[0], edge_tiles_out.at[0]),
            (tiles.at[blocks - 1], edge_tiles_out.at[1]),
        ],
        stores,
    )
    coarse_rows[...] = rows_split(inverse_rows[...])
    basis_columns[...] = parts.astype(jnp.float32).T.astype(jnp.bfloat16)
    for copy in copies:
        copy.wait()


def inner_sweeps_kernel(tiles, tiles_own, start, out, first_ends):
    blocks, nodes, _ = start.shape
    parts = [columns_split(start[b]) for b in range(blocks)]
    nothing = jnp.zeros_like(parts[0])
    for sweep in range(SWEEPS - 1):
        new = [
            start[b]
            + tile_product(
                tiles[b],
                tiles_own[b],
                parts[b - 1] if b else nothing,
                parts[b + 1] if b + 1 < blocks else nothing,
                parts[b],
            )
            for b in range(blocks)
        ]
        if sweep == 0:
            first_ends[0], first_ends[1] = new[0], new[-1]
        if sweep < SWEEPS - 2:
            parts = [columns_split(value) for value in new]
    for b in range(blocks):
        out[b] = new[b]


def outer_sweeps_kernel(odd, tiles, tiles_own, start, inner, first_ends, far, near, far_tile, near_tile, out):
    blocks, nodes, _ = start.shape
    even = odd[1] == 0
    far_tile, near_tile = far_tile[-nodes:], near_tile[-nodes:]
    ends = (
        (0, 1, jnp.where(even, far[:nodes], near[:nodes]), jnp.where(even, far_tile, near_tile)),
        (blocks - 1, -1, jnp.where(even, near[:nodes], far[:nodes]), jnp.where(even, near_tile, far_tile)),
    )
    for at, (end, inward, beside, tile) in enumerate(ends):
        tile = rows_split(tile)

        def of_block(b, outer, own=None, deeper=None):
            lower, upper = tiles[b][:, :nodes], tiles[b][:, nodes:]
            total = product(lower if inward == 1 else upper, outer)
            if own is not None:
                total = total + pair_product(tiles_own[b], own)
            if deeper is not None:
                total = total + product(upper if inward == 1 else lower, deeper)
            return total

        def of_beside(edge, last):
            return beside + product(tile, jnp.concatenate([columns_split(edge), last], axis=0))

        one, two, three = end, end + inward, end + 2 * inward
        beside_0 = columns_split(beside)
        first = of_block(one, beside_0)
        beside_1 = columns_split(of_beside(start[one], beside_0))
        beside_2 = columns_split(of_beside(first_ends[at] + first, beside_1))
        first = columns_split(first)
        second = columns_split(of_block(one, beside_1, first))
        second_two = columns_split(of_block(two, first))
        out[one] = inner[one] + of_block(one, beside_2, second, second_two)
        out[two] = inner[two] + of_block(two, second, second_two)
        out[three] = inner[three] + of_block(three, second_two)
    for b in range(3, blocks - 3):
        out[b] = inner[b]


def update_kernel(odd, coarse_rows, gathered, basis_columns, local, update, near_face, far_face, near_block, far_block):
    blocks, nodes, _ = local.shape
    faces = near_face.shape[1]
    correction = columns_split(product(coarse_rows[...], columns_split(gathered[...])))
    for b in range(blocks):
        new = local[b] + pair_product(basis_columns[b * nodes : (b + 1) * nodes], correction)
        update[b] = new
        south, north = new[:faces], new[nodes - faces :]
        even = odd[0] == 0
        near_face[b] = jnp.where(even, north, south)
        far_face[b] = jnp.where(even, south, north)
    even = odd[1] == 0
    near_block[...] = jnp.where(even, update[blocks - 1], update[0])
    far_block[...] = jnp.where(even, update[0], update[blocks - 1])


def keeping_update_kernel(odd, coarse_rows, gathered, basis_columns, local, far, near, update, near_face, far_face, near_block, far_block, far_kept, near_kept, sems):
    nodes = local.shape[1]
    copies = start_all([(far.at[nodes : 2 * nodes], far_kept), (near.at[nodes : 2 * nodes], near_kept)], sems)
    update_kernel(
        odd, coarse_rows, gathered, basis_columns, local, update, near_face, far_face, near_block, far_block
    )
    for copy in copies:
        copy.wait()


def linear_kernel(tiles, tiles_own, update, out):
    blocks = update.shape[0]
    parts = [columns_split(update[b]) for b in range(blocks)]
    nothing = jnp.zeros_like(parts[0])
    for b in range(blocks):
        before = parts[b - 1] if b else nothing
        after = parts[b + 1] if b + 1 < blocks else nothing
        out[b] = tile_product(tiles[b], tiles_own[b], before, after, parts[b])


def image_blocks(odd, edge_tiles, sides, linear, near_face, far_face, near_block, far_block):
    blocks, nodes, _ = linear.shape
    faces = near_face.shape[2]
    even = odd[1] == 0
    low = columns_split(jnp.where(even, far_block[...], near_block[...]))
    high = columns_split(jnp.where(even, near_block[...], far_block[...]))
    even = odd[0] == 0
    for b in range(blocks):
        new = linear[b]
        if b == 0:
            new = new + product(edge_tiles[0][:, :nodes], low)
        if b == blocks - 1:
            new = new + product(edge_tiles[1][:, nodes:], high)
        below = jnp.where(even, far_face[b], near_face[0, b])
        above = jnp.where(even, near_face[1, b], far_face[b])
        yield b, jnp.concatenate(
            [
                new[:faces] + sides[b, :faces] * below,
                new[faces : nodes - faces],
                new[nodes - faces :] + sides[b, faces:] * above,
            ],
            axis=0,
        )


def send_out(projected, spread, sems):
    return start_all([(projected, spread.at[i]) for i in range(spread.shape[0])], sems)


def image_kernel(odd, edge_tiles, sides, basis_rows, pair, residual, linear, far_face, near_face, near_block, far_block, image_out, rest_out, spread, start, near, far, image, rest, flat, projected, edges, sems, stores):
    blocks, nodes, _ = linear.shape
    for b, new in image_blocks(odd, edge_tiles, sides, linear, near_face, far_face, near_block, far_block):
        image[b] = new
        left = residual[b] - new
        rest[b] = left
        flat[b * nodes : (b + 1) * nodes] = columns_split(left)
    projected[...] = product(basis_rows[...], flat[...])
    copies = send_out(projected, spread, sems)
    for b in (0, blocks - 1, *range(1, blocks - 1)):
        start[b] = product(rows_split(pair[b][:, nodes:]), flat[b * nodes : (b + 1) * nodes])
        if b == blocks - 1:
            even = odd[1] == 0
            edges[0] = jnp.where(even, start[blocks - 1], start[0])
            edges[1] = jnp.where(even, start[0], start[blocks - 1])
            copies += start_all(
                [(edges.at[0], near), (edges.at[1], far), (image, image_out), (rest, rest_out)], stores
            )
    for copy in copies:
        copy.wait()


def project_kernel(basis_in, field_in, spread, basis, field, projected, sems, arrived):
    blocks, nodes, columns = field.shape
    third = blocks // 3
    loads = start_all(
        [(basis_in, basis)]
        + [(field_in.at[at : at + third], field.at[at : at + third]) for at in range(0, blocks, third)],
        arrived,
    )
    loads[0].wait()
    parts = []
    for i in range(3):
        loads[i + 1].wait()
        rows = rows_split(basis[:, i * third * nodes : (i + 1) * third * nodes])
        values = field[i * third : (i + 1) * third].reshape(third * nodes, columns)
        parts.append(product(rows, columns_split(values)))
    projected[...] = parts[0] + parts[1] + parts[2]
    for copy in send_out(projected, spread, sems):
        copy.wait()


def sums_kernel(odd, edge_tiles, sides, image, rest, linear, far_face, near_face, near_block, far_block, sums):
    nodes, columns = linear.shape[1:]
    parts = [jnp.zeros((8, columns), jnp.float32) for _ in range(5)]

    def inner(left, right):
        return jnp.sum((left * right).reshape(nodes // 8, 8, columns), axis=0)

    for b, new in image_blocks(odd, edge_tiles, sides, linear, near_face, far_face, near_block, far_block):
        change = new * SCALE
        left, right = image[b], rest[b]
        for i, (x, y) in enumerate(((left, right), (left, left), (change, right), (change, left), (change, change))):
            parts[i] = parts[i] + inner(x, y)
    for i in range(5):
        sums[i : i + 1] = jnp.sum(parts[i], axis=0, keepdims=True)


def call(kernel, outs, scratch, *operands, slow=0):
    specs, given = [], []
    for at, operand in enumerate(operands):
        space = pltpu.HBM if at >= len(operands) - slow else pltpu.VMEM
        if operand.dtype == jnp.int32:
            space = pltpu.SMEM
        elif operand.size > 2 * operand.shape[-1] ** 2 or space is pltpu.HBM:
            operand = pltpu.with_memory_space_constraint(operand, space)
        specs.append(pl.BlockSpec(memory_space=space))
        given.append(operand)
    return pl.pallas_call(
        kernel,
        out_shape=[(space or jax.ShapeDtypeStruct)(shape, kind) for shape, kind, space in outs],
        in_specs=specs,
        out_specs=[pl.BlockSpec(memory_space=space or pltpu.VMEM) for _, _, space in outs],
        scratch_shapes=scratch,
        compiler_params=pltpu.CompilerParams(vmem_limit_bytes=12 << 20),
        cost_estimate=pl.CostEstimate(flops=1000, transcendentals=0, bytes_accessed=1000),
    )(*given)


def shards(forcing, coupling, diag_pair, side, basis, coarse_inverse):
    residual = forcing[0]
    basis_all = basis[0]
    blocks, nodes, columns = residual.shape
    faces = side.shape[2] // 2
    coarse, own_coarse = coarse_inverse.shape[2], coarse_inverse.shape[1]
    odd = jnp.stack([lax.axis_index("sec") % 2, lax.axis_index("sub") % 2]).astype(jnp.int32)
    wide, thin, fast = jnp.float32, jnp.bfloat16, pltpu.VMEM
    subs = lax.axis_size("sub")
    block = ((nodes, columns), wide, None)
    edge = ((nodes, columns), wide, pltpu.HBM)
    small = ((2 * nodes, columns), wide, None)
    field = ((blocks, nodes, columns), wide, fast)
    kept = ((blocks, nodes, columns), wide, pltpu.HBM)
    face = ((blocks, faces, columns), wide, fast)
    tile = ((blocks, 2 * nodes, 2 * nodes), thin)
    tile_own = ((blocks, nodes, 2 * nodes), thin)
    spread_out = ((subs, own_coarse, columns), wide, pltpu.HBM)
    spreading = [pltpu.VMEM((own_coarse, columns), wide), pltpu.SemaphoreType.DMA((subs,))]

    (spread,) = call(
        project_kernel,
        [spread_out],
        [
            pltpu.VMEM(basis_all.shape, wide),
            pltpu.VMEM((blocks, nodes, columns), wide),
            *spreading,
            pltpu.SemaphoreType.DMA((4,)),
        ],
        basis_all, residual,
        slow=2,
    )
    spread, odd, residual, coupling, diag_pair, side, basis_all = lax.optimization_barrier(
        (spread, odd, residual, coupling, diag_pair, side, basis_all)
    )
    pair = diag_pair[0]
    near, far = call(
        edge_kernel,
        [small, small],
        [pltpu.VMEM((2, nodes, columns), wide)] * 3 + [pltpu.SemaphoreType.DMA((6,))],
        odd, coupling[0], pair, residual,
        slow=3,
    )
    halo = swap(near, far, "sub")
    sweep, sweep_own, tiles, tiles_own, edge_tiles, start, sides, basis_rows, basis_columns, coarse_rows = call(
        prepare_kernel,
        [
            (*tile, fast),
            (*tile_own, fast),
            (*tile, pltpu.HBM),
            (*tile_own, pltpu.HBM),
            ((2, 2 * nodes, 2 * nodes), thin, pltpu.HBM),
            field,
            ((blocks, 2 * faces, columns), wide, pltpu.HBM),
            ((2 * own_coarse, blocks * nodes), thin, pltpu.HBM),
            ((blocks * nodes, 2 * own_coarse), thin, fast),
            ((2 * own_coarse, coarse), thin, fast),
        ],
        [
            pltpu.VMEM((blocks, nodes, columns), wide),
            pltpu.VMEM((blocks, nodes, columns), wide),
            pltpu.VMEM((blocks, nodes, columns), wide),
            pltpu.VMEM(basis_all.shape, wide),
            pltpu.VMEM((own_coarse, coarse), wide),
            pltpu.VMEM(*tile),
            pltpu.VMEM(*tile_own),
            pltpu.VMEM((blocks, 2 * faces, columns), wide),
            pltpu.VMEM((2 * own_coarse, blocks * nodes), thin),
            pltpu.SemaphoreType.DMA((5,)),
            pltpu.SemaphoreType.DMA((6,)),
        ],
        side[0], coupling[0], pair, residual, basis_all, coarse_inverse[0],
        slow=5,
    )

    def precondition(start, near, far, kept, spread):
        gathered = gather_sub(spread)
        inner, first_ends = call(
            inner_sweeps_kernel, [field, ((2, nodes, columns), wide, None)], [], sweep, sweep_own, start
        )
        (local,) = call(
            outer_sweeps_kernel, [field], [], odd, sweep, sweep_own, start, inner, first_ends, far, near, *(kept or (far, near))
        )
        outs = [field, face, face, block, block]
        given = (odd, coarse_rows, gathered, basis_columns, local)
        if kept:
            update, near_face, far_face, near_block, far_block = call(update_kernel, outs, [], *given)
        else:
            update, near_face, far_face, near_block, far_block, *kept = call(
                keeping_update_kernel, [*outs, edge, edge], [pltpu.SemaphoreType.DMA((2,))], *given, far, near
            )
        sections = lax.axis_size("sec")
        pairs = [[i, i + 1] for i in range(0, sections, 2)]
        faces_in = (
            lax.all_gather(near_face, "sec", axis_index_groups=pairs),
            lax.ppermute(far_face, "sec", pairings("sec")[1]),
        )
        blocks_in = swap(near_block, far_block, "sub")
        (linear,) = call(linear_kernel, [field], [], tiles, tiles_own, update)
        return kept, update, linear, faces_in[1], faces_in[0], *blocks_in

    kept_tiles, first, linear, *given = precondition(start, *halo, None, spread)
    image, rest, spread, start, near, far = call(
        image_kernel,
        [kept, kept, spread_out, field, edge, edge],
        [
            pltpu.VMEM((blocks, nodes, columns), wide),
            pltpu.VMEM((blocks, nodes, columns), wide),
            pltpu.VMEM((blocks * nodes, 2 * columns), thin),
            pltpu.VMEM((own_coarse, columns), wide),
            pltpu.VMEM((2, nodes, columns), wide),
            pltpu.SemaphoreType.DMA((subs,)),
            pltpu.SemaphoreType.DMA((4,)),
        ],
        odd, edge_tiles, sides, basis_rows, pair, residual, linear, *given,
    )
    _, second, linear, *given = precondition(start, *swap(near, far, "sub"), kept_tiles, spread)
    (sums,) = call(sums_kernel, [((5, columns), wide, fast)], [], odd, edge_tiles, sides, image, rest, linear, *given)
    sums = total(sums)
    short = -sums[0] / sums[1]
    step = 1.0 - short
    upper = step * (sums[2] + short * sums[3])
    scaled = step / SCALE
    lower = short * short * sums[1] + 2.0 * short * scaled * sums[3] + scaled * scaled * sums[4]
    step_next = upper / SCALE / lower
    result = (step + step_next * short) * first + (step_next * step) * second
    return result[None]


def solution(mesh):
    placed = (
        P("sec", "sub", None, None),
        P("sec", "sub", None, None),
        P("sec", "sub", None, None),
        P("sec", "sub", None),
        P("sec", "sub", None),
        P("sec", "sub", None),
    )
    return jax.shard_map(
        shards, mesh=mesh, in_specs=placed, out_specs=P("sec", "sub", None, None), check_vma=False
    )
```
